128 devices in a mesh: dp: 8 (over z, y_lo), ctx: 8 (over x, y_hi), tp: 2 (over core).
Axes of the slice: x: 4, y: 4 (y_hi: 2, y_lo: 2; y = y_hi * 2 + y_lo), z: 4, core: 2. Of those that a mesh axis runs over, the one named last changes fastest.
Arguments:
- hidden_in: bfloat16 [16, 1024, 1536], P('dp', 'ctx'), may hold values from -6 to 6
- context: bfloat16 [16, 130, 1536], P('dp'), may hold values from -6 to 6
- lengths: int32 [16], P('dp'), may hold values from 128 to 1024, as said below
- cond_mask: int32 [16, 130], P('dp'), may hold values from 0 to 1, as said below
- out_grad: bfloat16 [16, 1024, 1536], P('dp', 'ctx'), may hold values from -6 to 6
- gain_attn: bfloat16 [1536], P('dp'), may hold values from 0.099609375 to 1.8984375
- self_proj: bfloat16 [1536, 3, 1536], P('dp', None, 'tp')
- self_out: bfloat16 [1536, 1536], P('dp', 'tp'), may hold values from -2.5 to 2.5
- gain_cross: bfloat16 [1536], P('dp'), may hold values from 0.099609375 to 1.8984375
- cross_query: bfloat16 [1536, 1536], P('dp', 'tp'), may hold values from -0.15625 to 0.15625
- cross_keyval: bfloat16 [1536, 2, 1536], P('dp', None, 'tp'), may hold values from -0.15625 to 0.15625
- cross_out: bfloat16 [1536, 1536], P('dp', 'tp'), may hold values from -0.875 to 0.875
- gain_feed: bfloat16 [1536], P('dp'), may hold values from 0.099609375 to 1.8984375
- feed_in: bfloat16 [1536, 2, 6144], P('dp', None, 'tp'), may hold values from -0.15625 to 0.15625
- feed_out: bfloat16 [1536, 6144], P('dp', 'tp'), may hold values from -0.078125 to 0.078125
Outputs:
- layer_out: bfloat16 [16, 1024, 1536], P('dp', 'ctx')
- in_grad: float32 [16, 1024, 1536], P('dp', 'ctx')
- cond_grad: float32 [16, 130, 1536], P('dp')
- layer_stats: float32 [16, 5], P('dp')
- grad_gain_attn: float32 [1536], P('dp')
- grad_self_proj: float32 [1536, 3, 1536], P('dp', None, 'tp')
- grad_self_out: float32 [1536, 1536], P('dp', 'tp')
- grad_gain_cross: float32 [1536], P('dp')
- grad_cross_query: float32 [1536, 1536], P('dp', 'tp')
- grad_cross_keyval: float32 [1536, 2, 1536], P('dp', None, 'tp')
- grad_cross_out: float32 [1536, 1536], P('dp', 'tp')
- grad_gain_feed: float32 [1536], P('dp')
- grad_feed_in: float32 [1536, 2, 6144], P('dp', None, 'tp')
- grad_feed_out: float32 [1536, 6144], P('dp', 'tp')
The draws below stay inside these ranges and needn't reach their ends.
Inputs may be any that keep to these rules, and one draw needn't show every extreme that they name: `lengths`: one sequence has exactly 1024 valid tokens. `cond_mask`: the first conditioning token of every sequence is valid.
All inputs are finite; a program needn't handle non-finite values.
Results may differ from the reference program's by a relative error of at most 0.025.
Values may be sent and summed in bfloat16 or wider, within the bound.
No kernel may reach another device: no remote copies, remote signals or barrier semaphores. Data moves between devices by JAX's collectives and lax.ppermute only.
A program may use at most 256 MiB of HBM per device.

```python
import jax
import jax.numpy as jnp
from jax import lax

H = 24
HD = 64
ROT = 32
D = 1536
FF = 6144
CD = 1536
CT = 130
SEQ_LEN = 1024
SEQS = 16


def draw_lengths(key, part):
    drawn = jax.random.randint(key, (SEQS,), SEQ_LEN // 8, SEQ_LEN + 1, dtype=jnp.int32)
    longest = jax.random.randint(jax.random.fold_in(key, 7), (), 0, SEQS, dtype=jnp.int32)
    return drawn.at[longest].set(SEQ_LEN)


def draw_cond_mask(key, part):
    drawn = jax.random.randint(key, (SEQS, CT), 0, 4, dtype=jnp.int32)
    kept = jnp.minimum(drawn, 1)
    return kept.at[:, 0].set(1)


def draw_self_proj(key, part):
    entries = jax.random.truncated_normal(jax.random.fold_in(key, 11), -3.0, 3.0, (D, 3, D), jnp.float32)
    columns = jax.random.truncated_normal(jax.random.fold_in(key, 12), -3.0, 3.0, (1, 3, D), jnp.float32)
    return ((entries + 0.5 * columns) * D ** (-0.5)).astype(jnp.bfloat16)


def level_of(stream_key, dims, shards, least, largest):
    loudness, own = 1.0, jax.random.fold_in(stream_key, 6)
    for dim, shards_of in shards:
        heights = jnp.exp(jax.random.uniform(jax.random.fold_in(own, dim), (shards_of,), jnp.float32, least / len(shards), largest / len(shards)))
        loudness = loudness * jnp.repeat(heights, dims[dim] // shards_of).reshape([-1 if axis == dim else 1 for axis in range(len(dims))])
    return loudness


def centred(rng, extent, width, bound, pieces=(), kind=jnp.bfloat16):
    values = jax.random.normal(rng, extent, jnp.float32) * width
    if len(pieces) > 0:
        values = level_of(rng, extent, pieces, -0.22, 0.18) * values
    return jnp.clip(values, min=-bound, max=bound).astype(kind)


def setup_inputs(seed: int = 0) -> dict:
    splits = jax.random.split(jax.random.key(seed), 16)
    hidden_in = centred(splits[0], (SEQS, SEQ_LEN, D), 1.0, 6.0, ((0, 8), (1, 8)))
    context = centred(splits[1], (SEQS, CT, CD), 1.0, 6.0, ((0, 8),))
    lengths = draw_lengths(jax.random.fold_in(splits[15], 71), 0)
    cond_mask = draw_cond_mask(jax.random.fold_in(splits[15], 71), 0)
    out_grad = centred(splits[4], (SEQS, SEQ_LEN, D), 1.0, 6.0, ((0, 8), (1, 8)))
    gain_attn = jnp.clip(1.0 + 0.18 * jax.random.normal(splits[5], (D,), jnp.float32), 0.099609375, 1.8984375).astype(jnp.bfloat16)
    self_proj = draw_self_proj(jax.random.fold_in(splits[15], 71), 0)
    self_out = centred(splits[7], (D, D), (max(4 * D // SEQ_LEN, 1)) ** -0.5, 2.5, ((0, 8), (1, 2)))
    gain_cross = jnp.clip(1.0 + 0.18 * jax.random.normal(splits[8], (D,), jnp.float32), 0.099609375, 1.8984375).astype(jnp.bfloat16)
    cross_query = centred(splits[9], (D, D), D ** -0.5, 0.15625, ((0, 8), (1, 2)))
    cross_keyval = centred(splits[10], (CD, 2, D), CD ** -0.5, 0.15625, ((0, 8), (2, 2)))
    cross_out = centred(splits[11], (D, D), (max(D // 32, 1)) ** -0.5, 0.875, ((0, 8), (1, 2)))
    gain_feed = jnp.clip(1.0 + 0.18 * jax.random.normal(splits[12], (D,), jnp.float32), 0.099609375, 1.8984375).astype(jnp.bfloat16)
    feed_in = centred(splits[13], (D, 2, FF), D ** -0.5, 0.15625, ((0, 8), (2, 2)))
    feed_out = centred(splits[14], (D, FF), FF ** -0.5, 0.078125, ((0, 8), (1, 2)))
    return dict(hidden_in=hidden_in, context=context, lengths=lengths, cond_mask=cond_mask, out_grad=out_grad, gain_attn=gain_attn, self_proj=self_proj, self_out=self_out, gain_cross=gain_cross, cross_query=cross_query, cross_keyval=cross_keyval, cross_out=cross_out, gain_feed=gain_feed, feed_in=feed_in, feed_out=feed_out)


@jax.custom_vjp
def low(v):
    return lax.optimization_barrier(v.astype(jnp.bfloat16)).astype(jnp.float32)

@jax.custom_vjp
def low_back(v):
    return v

def low_keep(v):
    return (low(v), None)

def low_pass(kept, grad):
    return (grad,)

def back_keep(v):
    return (v, None)

def back_low(kept, grad):
    return (low(grad),)
low.defvjp(low_keep, low_pass)
low_back.defvjp(back_keep, back_low)
norm_eps = 1e-05
masked_fill = -1e+30
highest = lax.Precision.HIGHEST

def layer_norm(field_in, gain_vec):
    average = lax.optimization_barrier(jnp.mean(field_in, axis=-1, keepdims=True))
    centered = field_in - average
    variance = lax.optimization_barrier(jnp.mean(centered * centered, axis=-1, keepdims=True))
    return centered * lax.rsqrt(variance + norm_eps) * gain_vec

def rotate_half(vector):
    half_size = vector.shape[-1] // 2
    return jnp.concatenate([-vector[..., half_size:], vector[..., :half_size]], axis=-1)

def rotary_tables(first_row, number_rows, turned_size):
    positions = (first_row + jnp.arange(number_rows, dtype=jnp.int32)).astype(jnp.float32)
    exponent = jnp.arange(turned_size // 2, dtype=jnp.int32).astype(jnp.float32) * (2.0 / turned_size)
    frequency = jnp.power(jnp.float32(10000.0), -exponent)
    angles = positions[:, None] * frequency[None, :]
    angles = jnp.concatenate([angles, angles], axis=-1)
    return (jnp.cos(angles), jnp.sin(angles))

def rotate(vector, cosine_table, sine_table):
    turned_size = cosine_table.shape[-1]
    turned = vector[..., :turned_size]
    turned = turned * cosine_table + rotate_half(turned) * sine_table
    return jnp.concatenate([turned, vector[..., turned_size:]], axis=-1)

def softmax_rows(scores, valid_mask):
    masked = jnp.where(valid_mask, scores, masked_fill)
    maximum = lax.optimization_barrier(jnp.max(masked, axis=-1, keepdims=True))
    exponent = jnp.exp(masked - maximum)
    row_total = lax.optimization_barrier(jnp.sum(exponent, axis=-1, keepdims=True))
    return (exponent / row_total, maximum + jnp.log(row_total))

def glu_unit(gate_part, upward):
    return gate_part * jax.nn.sigmoid(gate_part) * upward

def sequence_forward(token_rows, cond_rows, weight_set, length, cond_valid):
    gain_one, self_proj, self_out, gain_two, cross_query, cross_keyval, cross_out, gain_three, feed_in, feed_out = weight_set
    seq_len = token_rows.shape[0]
    head_scale = HD ** (-0.5)
    normed_one = low(layer_norm(token_rows, gain_one))
    projected = jnp.dot(normed_one, self_proj.reshape(D, 3 * D), precision=highest).reshape(seq_len, 3, H, HD)
    cosine_table, sine_table = rotary_tables(0, seq_len, ROT)
    cosine_table = cosine_table[:, None, :]
    sine_table = sine_table[:, None, :]
    queries = low(rotate(low_back(projected[:, 0]), cosine_table, sine_table) * head_scale)
    rotated_keys = low(rotate(low_back(projected[:, 1]), cosine_table, sine_table))
    value_rows = low(low_back(projected[:, 2]))
    key_valid = jnp.arange(seq_len) < length
    scores = low_back(jnp.einsum('qhe,khe->hqk', queries, rotated_keys, precision=highest))
    attn_probs = low(softmax_rows(scores, key_valid[None, None, :])[0])
    attended = low(low_back(jnp.einsum('hqk,khe->qhe', attn_probs, value_rows, precision=highest))).reshape(seq_len, D)
    attn_branch = low_back(jnp.dot(attended, self_out.T, precision=highest))
    resid_one = token_rows + attn_branch
    normed_two = low(layer_norm(resid_one, gain_two))
    cross_q = low(low_back(jnp.dot(normed_two, cross_query, precision=highest)) * head_scale).reshape(seq_len, H, HD)
    cond_proj = jnp.dot(cond_rows, cross_keyval.reshape(CD, 2 * D), precision=highest).reshape(CT, 2, H, HD)
    cross_k = low(low_back(cond_proj[:, 0]))
    cross_v = low(low_back(cond_proj[:, 1]))
    cross_scores = low_back(jnp.einsum('qhe,khe->hqk', cross_q, cross_k, precision=highest))
    cross_probs = low(softmax_rows(cross_scores, (cond_valid > 0)[None, None, :])[0])
    cross_att = low(low_back(jnp.einsum('hqk,khe->qhe', cross_probs, cross_v, precision=highest))).reshape(seq_len, D)
    cross_branch = low_back(jnp.dot(cross_att, cross_out.T, precision=highest))
    resid_two = resid_one + cross_branch
    normed_three = low(layer_norm(resid_two, gain_three))
    gate_up = jnp.dot(normed_three, feed_in.reshape(D, 2 * FF), precision=highest).reshape(seq_len, 2, FF)
    hidden = low(glu_unit(low_back(gate_up[:, 0]), low_back(gate_up[:, 1])))
    feed_branch = low_back(jnp.dot(hidden, feed_out.T, precision=highest))
    output = resid_two + feed_branch
    return (output, (attn_branch, cross_branch, feed_branch))

def valid_rms(fields, length):
    valid_rows = jnp.arange(fields[0].shape[0]) < length
    square_sums = jnp.stack([jnp.sum(jnp.where(valid_rows[:, None], field_in * field_in, 0.0)) for field_in in fields])
    return jnp.sqrt(square_sums / (length.astype(jnp.float32) * D))

def reference(hidden_in, context, lengths, cond_mask, out_grad, gain_attn, self_proj, self_out, gain_cross, cross_query, cross_keyval, cross_out, gain_feed, feed_in, feed_out):
    weights = tuple((weight.astype(jnp.float32) for weight in (gain_attn, self_proj, self_out, gain_cross, cross_query, cross_keyval, cross_out, gain_feed, feed_in, feed_out)))

    def one_sequence(carried, inputs):
        token_rows, cond_rows, length, cond_valid, cotangent = inputs

        def forward(token_part, cond_part, weight_set):
            return sequence_forward(token_part, cond_part, weight_set, length, cond_valid)
        output, pullback, branches = jax.vjp(forward, token_rows.astype(jnp.float32), cond_rows.astype(jnp.float32), weights, has_aux=True)
        grad_tokens, grad_cond, grad_weights = pullback(cotangent.astype(jnp.float32))
        carried = tuple((running + update for running, update in zip(carried, grad_weights)))
        stat_row = valid_rms((token_rows.astype(jnp.float32),) + branches + (output,), length)
        return (carried, (output.astype(jnp.bfloat16), grad_tokens, grad_cond, stat_row))
    zero_grads = tuple((jnp.zeros(weight.shape, jnp.float32) for weight in weights))
    totals, stacked = lax.scan(one_sequence, zero_grads, (hidden_in, context, lengths, cond_mask, out_grad))
    return (stacked[0], stacked[1], stacked[2], stacked[3], totals[0], totals[1], totals[2], totals[3], totals[4], totals[5], totals[6], totals[7], totals[8], totals[9])
```

```python
import jax
import jax.numpy as jnp
from jax import lax
from jax.experimental import pallas as pl
from jax.experimental.pallas import tpu as pltpu
from jax.sharding import Mesh
from jax.sharding import PartitionSpec as P

DP = ("z", "yl")
CTX = ("x", "yh")
PLANE = ("z", "yh", "yl")
SWAP = ((0, 0), (1, 2), (2, 1), (3, 3))

D = 1536
HD = 64
ROT = 32
HEADS = 3
WIDE = 256
ROWS = 128
SEQ = 1024
QB = 256
CROSS_KEYS = 144
norm_eps = 1e-05
masked_fill = -1e30
bf16 = jnp.bfloat16
f32 = jnp.float32


def permuted(v):
    parts = []
    for z in range(4):
        for piece in (0, 2, 1, 3):
            at = z * 384 + piece * 96
            parts.append(v[..., at : at + 96])
    return jnp.concatenate(parts, axis=-1)


def dot(a, b):
    return jnp.dot(a, b, preferred_element_type=f32)


def dot_nt(a, b):
    return lax.dot_general(a, b, (((1,), (1,)), ((), ())), preferred_element_type=f32)


def dot_tn(a, b):
    return lax.dot_general(a, b, (((0,), (0,)), ((), ())), preferred_element_type=f32)


def to_partner(v):
    return lax.ppermute(v, "tp", ((0, 1), (1, 0)))


def sent_to_all(v, axes, count):
    copies = jnp.broadcast_to(v[None], (count, *v.shape))
    return lax.all_to_all(copies, axes, split_axis=0, concat_axis=0, tiled=True)


def gather_rows(own):
    mine = sent_to_all(own, "x", 4).reshape(4 * ROWS, D)
    return jnp.concatenate([mine, to_partner(mine)], axis=0)


def scatter_rows(partial):
    half = 4 * ROWS
    got = to_partner(partial[half:].astype(bf16))
    mine = (partial[:half] + got.astype(f32)).astype(bf16)
    arrived = lax.all_to_all(mine.reshape(4, ROWS, D), "x", split_axis=0, concat_axis=0, tiled=True)
    return jnp.sum(arrived.astype(f32), axis=0)


def pair_rows(own):
    return jnp.concatenate([own, to_partner(own)], axis=0)


def pair_sum(partial):
    return partial[:ROWS] + to_partner(partial[ROWS:])


def gather_plane(shard):
    return lax.all_gather(shard, PLANE, axis=0, tiled=True)


def scatter_plane(grad):
    return lax.psum_scatter(grad, PLANE, scatter_dimension=0, tiled=True)


def unit_norm(v):
    centered = v - jnp.mean(v, axis=-1, keepdims=True)
    scale = lax.rsqrt(jnp.mean(centered * centered, axis=-1, keepdims=True) + norm_eps)
    return centered * scale, scale


def unit_norm_back(x_hat, scale, grad):
    along = jnp.mean(grad * x_hat, axis=-1, keepdims=True)
    return scale * (grad - jnp.mean(grad, axis=-1, keepdims=True) - x_hat * along)


def lane_masks(rows):
    lane = lax.broadcasted_iota(jnp.int32, (rows, WIDE), 1)
    heads = [(lane // HD == h).astype(f32).astype(bf16) for h in range(HEADS)]
    return lane, heads, (lane == HEADS * HD).astype(f32).astype(bf16)


def turned(v, cosine, sine, first):
    other = jnp.where(first, pltpu.roll(v, WIDE - ROT // 2, 1), pltpu.roll(v, ROT // 2, 1))
    return v * cosine, other * sine


def attn_forward_kernel(sc, qkv, cosine, sine, att, qs, ks, vs, lse, vt):
    lane, heads, extra = lane_masks(QB)
    first = lane % HD < ROT // 2
    wide_head = lax.broadcasted_iota(jnp.int32, (WIDE, QB), 0) // HD

    def prepare(block, carry):
        rows = pl.ds(block * QB, QB)
        c, s = cosine[rows, :], sine[rows, :]
        straight, crossed = turned(qkv[rows, 0:WIDE], c, s, first)
        query = ((straight + crossed) * HD ** (-0.5)).astype(bf16)
        qs[rows, :] = jnp.where(lane < HEADS * HD, query.astype(f32), jnp.where(lane == HEADS * HD, 1.0, 0.0)).astype(bf16)
        straight, crossed = turned(qkv[rows, WIDE : 2 * WIDE], c, s, first)
        row = lax.broadcasted_iota(jnp.int32, (QB, WIDE), 0) + block * QB
        side = jnp.where(row < SEQ // 2, sc[0], 1 - sc[0])
        within = row % (SEQ // 2)
        place = (within // ROWS * 2 + side) * ROWS + within % ROWS
        fill = jnp.where((lane == HEADS * HD) & (place >= sc[1]), masked_fill, 0.0)
        ks[rows, :] = jnp.where(lane < HEADS * HD, straight + crossed, fill).astype(bf16)
        value = qkv[rows, 2 * WIDE : 3 * WIDE]
        vs[rows, :] = value.astype(bf16)
        vt[:, rows] = value.T.astype(bf16)
        return carry

    for block in range(SEQ // QB):
        prepare(block, 0)

    def attend(block, carry):
        rows = pl.ds(pl.multiple_of(block * QB, QB), QB)
        query = qs[rows, :]
        total = jnp.zeros((WIDE, QB), f32)
        for h in range(HEADS):
            scores = dot_nt(ks[...], query * (heads[h] + extra))
            top = jnp.max(scores, axis=0, keepdims=True)
            weight = jnp.exp(scores - top)
            mass = jnp.sum(weight, axis=0, keepdims=True)
            out = dot(vt[...], weight.astype(bf16))
            total = jnp.where(wide_head == h, out / mass, total)
            lse[h : h + 1, rows] = top + jnp.log(mass)
        att[rows, :] = total.T.astype(bf16)
        return carry

    lse[...] = jnp.zeros(lse.shape, f32)
    lax.fori_loop(0, SEQ // QB, attend, 0)


def attn_forward(scalars, qkv, cosine, sine):
    wide = jax.ShapeDtypeStruct((SEQ, WIDE), bf16)
    return pl.pallas_call(
        attn_forward_kernel,
        in_specs=[pl.BlockSpec(memory_space=pltpu.SMEM)] + [pl.BlockSpec(memory_space=pltpu.VMEM)] * 3,
        out_shape=(wide, wide, wide, wide, jax.ShapeDtypeStruct((8, SEQ), f32)),
        scratch_shapes=[pltpu.VMEM((WIDE, SEQ), bf16)],
        cost_estimate=pl.CostEstimate(flops=4 * HEADS * SEQ * SEQ * WIDE, transcendentals=HEADS * SEQ * SEQ, bytes_accessed=8 << 20),
    )(scalars, qkv, cosine, sine)


def attn_backward_kernel(qs, ks, vs, grad, lse, cosine, sine, out, kt, dk, dv):
    lane, heads, extra = lane_masks(QB)
    first = lane % HD < ROT // 2
    wide_head = lax.broadcasted_iota(jnp.int32, (WIDE, QB), 0) // HD
    kept = lane < HEADS * HD
    kt[...] = ks[...].astype(f32).T.astype(bf16)
    dk[...] = jnp.zeros(dk.shape, f32)
    dv[...] = jnp.zeros(dv.shape, f32)

    def step(block, carry):
        rows = pl.ds(pl.multiple_of(block * QB, QB), QB)
        query, given = qs[rows, :], grad[rows, :]
        total = jnp.zeros((WIDE, QB), f32)
        for h in range(HEADS):
            own_query, own_grad = query * heads[h], given * heads[h]
            scores = dot_nt(ks[...], query * (heads[h] + extra))
            weight = jnp.exp(scores - lse[h : h + 1, rows])
            wanted = dot_nt(vs[...], own_grad)
            product = weight * wanted
            inner = jnp.sum(product, axis=0, keepdims=True)
            slope = (product - weight * inner).astype(bf16)
            dv[...] += dot(weight.astype(bf16), own_grad)
            dk[...] += dot(slope, own_query)
            total = jnp.where(wide_head == h, dot(kt[...], slope), total)
        straight, crossed = turned(total.T * HD ** (-0.5), cosine[rows, :], sine[rows, :], first)
        out[rows, 0:WIDE] = jnp.where(kept, straight - crossed, 0.0).astype(bf16)
        return carry

    lax.fori_loop(0, SEQ // QB, step, 0)
    for block in range(SEQ // QB):
        rows = pl.ds(block * QB, QB)
        straight, crossed = turned(dk[rows, :], cosine[rows, :], sine[rows, :], first)
        out[rows, WIDE : 2 * WIDE] = jnp.where(kept, straight - crossed, 0.0).astype(bf16)
        out[rows, 2 * WIDE : 3 * WIDE] = dv[rows, :].astype(bf16)


def attn_backward(qs, ks, vs, grad, lse, cosine, sine):
    return pl.pallas_call(
        attn_backward_kernel,
        in_specs=[pl.BlockSpec(memory_space=pltpu.VMEM)] * 7,
        out_shape=jax.ShapeDtypeStruct((SEQ, 3 * WIDE), bf16),
        scratch_shapes=[pltpu.VMEM((WIDE, SEQ), bf16), pltpu.VMEM((SEQ, WIDE), f32), pltpu.VMEM((SEQ, WIDE), f32)],
        cost_estimate=pl.CostEstimate(flops=10 * HEADS * SEQ * SEQ * WIDE, transcendentals=HEADS * SEQ * SEQ, bytes_accessed=8 << 20),
    )(qs, ks, vs, grad, lse, cosine, sine)


PAIR = 2 * HD


def cross_weights(query, keys, bias):
    scores = dot_nt(keys, query) + bias
    weight = jnp.exp(scores - jnp.max(scores, axis=0, keepdims=True))
    return weight / jnp.sum(weight, axis=0, keepdims=True)


def cross_forward_kernel(cq, ck, cv, bias, att):
    lane = lax.broadcasted_iota(jnp.int32, (2 * ROWS, PAIR), 1)
    row = lax.broadcasted_iota(jnp.int32, (PAIR, 2 * ROWS), 0)
    for group in range(cq.shape[1] // PAIR):
        at = pl.ds(group * PAIR, PAIR)
        query, keys = cq[:, at], ck[:, at]
        values = cv[:, at].astype(f32).T.astype(bf16)
        outs = []
        for h in range(2):
            mask = (lane // HD == h).astype(f32).astype(bf16)
            weight = cross_weights(query * mask, keys, bias[...])
            outs.append(dot(values, weight.astype(bf16)))
        att[:, at] = jnp.where(row < HD, outs[0], outs[1]).T.astype(bf16)


def cross_forward(cq, ck, cv, bias):
    return pl.pallas_call(
        cross_forward_kernel,
        in_specs=[pl.BlockSpec(memory_space=pltpu.VMEM)] * 4,
        out_shape=jax.ShapeDtypeStruct(cq.shape, bf16),
        cost_estimate=pl.CostEstimate(flops=4 * 12 * 256 * 144 * 128, transcendentals=12 * 256 * 144, bytes_accessed=2 << 20),
    )(cq, ck, cv, bias)


def cross_backward_kernel(cq, ck, cv, bias, grad, dq, dkv):
    lane = lax.broadcasted_iota(jnp.int32, (2 * ROWS, PAIR), 1)
    row = lax.broadcasted_iota(jnp.int32, (PAIR, 2 * ROWS), 0)
    width = cq.shape[1]
    for group in range(width // PAIR):
        at = pl.ds(group * PAIR, PAIR)
        query, keys, values, given = cq[:, at], ck[:, at], cv[:, at], grad[:, at]
        turned_keys = keys.astype(f32).T.astype(bf16)
        outs, key_grad, value_grad = [], 0.0, 0.0
        for h in range(2):
            mask = (lane // HD == h).astype(f32).astype(bf16)
            own_query, own_grad = query * mask, given * mask
            weight = cross_weights(own_query, keys, bias[...])
            product = weight * dot_nt(values, own_grad)
            slope = (product - weight * jnp.sum(product, axis=0, keepdims=True)).astype(bf16)
            outs.append(dot(turned_keys, slope))
            key_grad += dot(slope, own_query)
            value_grad += dot(weight.astype(bf16), own_grad)
        dq[:, at] = (jnp.where(row < HD, outs[0], outs[1]).T * HD ** (-0.5)).astype(bf16)
        dkv[:, at] = key_grad.astype(bf16)
        dkv[:, pl.ds(width + group * PAIR, PAIR)] = value_grad.astype(bf16)


def cross_backward(cq, ck, cv, bias, grad):
    return pl.pallas_call(
        cross_backward_kernel,
        in_specs=[pl.BlockSpec(memory_space=pltpu.VMEM)] * 5,
        out_shape=(jax.ShapeDtypeStruct(cq.shape, bf16), jax.ShapeDtypeStruct((CROSS_KEYS, 2 * cq.shape[1]), bf16)),
        cost_estimate=pl.CostEstimate(flops=10 * 12 * 256 * 144 * 128, transcendentals=12 * 256 * 144, bytes_accessed=3 << 20),
    )(cq, ck, cv, bias, grad)


def rotary_lanes(side):
    row = jnp.arange(SEQ, dtype=jnp.int32)
    within = row % (SEQ // 2)
    part = jnp.where(row < SEQ // 2, side, 1 - side)
    place = ((within // ROWS * 2 + part) * ROWS + within % ROWS).astype(f32)
    lane = jnp.arange(WIDE, dtype=jnp.int32) % HD
    exponent = (lane % (ROT // 2)).astype(f32) * (2.0 / ROT)
    angle = place[:, None] * jnp.power(jnp.float32(10000.0), -exponent)[None, :]
    inside = (lane < ROT)[None, :]
    sign = jnp.where(lane < ROT // 2, -1.0, 1.0)[None, :]
    return jnp.where(inside, jnp.cos(angle), 1.0), jnp.where(inside, jnp.sin(angle) * sign, 0.0)


def per_device(
    hidden_in,
    context,
    lengths,
    cond_mask,
    out_grad,
    gain_attn,
    self_proj,
    self_out,
    gain_cross,
    cross_query,
    cross_keyval,
    cross_out,
    gain_feed,
    feed_in,
    feed_out,
):
    x, yh, tp = lax.axis_index("x"), lax.axis_index("yh"), lax.axis_index("tp")
    cond_count = context.shape[1]
    own_rows = hidden_in.shape[1]
    half_rows = self_proj.shape[0] // 2
    quarter = self_proj.shape[2] // 4
    hidden_quarter = feed_in.shape[2] // 4
    local_width = self_proj.shape[2]

    def own_half(w):
        return lax.dynamic_slice_in_dim(w, yh * half_rows, half_rows, 0)

    def own_cols(w, count):
        return lax.dynamic_slice_in_dim(w, x * count, count, w.ndim - 1)

    def scaled(w, gain):
        g = own_half(gain).astype(f32)
        return (w.astype(f32) * g.reshape((-1,) + (1,) * (w.ndim - 1))).astype(bf16)

    x_own = lax.ppermute(lax.dynamic_index_in_dim(hidden_in, tp, 0, False), ("yh", "tp"), SWAP)
    u_own = lax.ppermute(lax.dynamic_index_in_dim(out_grad, tp, 0, False), ("yh", "tp"), SWAP)
    length = lax.dynamic_index_in_dim(lengths, yh, 0, False)
    own_mask = lax.dynamic_index_in_dim(cond_mask, yh, 0, False)
    own_context = permuted(lax.dynamic_index_in_dim(context, yh, 0, False))

    proj_cols = scaled(own_cols(own_half(self_proj), quarter), gain_attn)
    proj_cols = jnp.pad(proj_cols, ((0, 0), (0, 0), (0, WIDE - quarter))).reshape(half_rows, 3 * WIDE)
    out_cols = jnp.pad(own_cols(own_half(self_out), quarter), ((0, 0), (0, WIDE - quarter)))
    attn_set = gather_plane(jnp.concatenate([proj_cols, out_cols], axis=1))
    keyval_cols = own_cols(own_half(cross_keyval), quarter).reshape(half_rows, 2 * quarter)
    cross_set = gather_plane(
        jnp.concatenate([scaled(own_half(cross_query), gain_cross), own_half(cross_out), keyval_cols], axis=1)
    )
    feed_cols = scaled(own_cols(own_half(feed_in), hidden_quarter), gain_feed).reshape(half_rows, 2 * hidden_quarter)
    w_feed = gather_plane(feed_cols)
    w_down = gather_plane(own_cols(own_half(feed_out), hidden_quarter))
    w_proj, w_out = attn_set[:, : 3 * WIDE], attn_set[:, 3 * WIDE :]
    w_cq = cross_set[:, :local_width]
    w_co = cross_set[:, local_width : 2 * local_width]
    w_kv = cross_set[:, 2 * local_width :]

    tokens = permuted(x_own).astype(f32)
    norm_one, scale_one = unit_norm(tokens)
    full_one = gather_rows(norm_one.astype(bf16))
    cosine, sine = rotary_lanes(tp)
    scalars = jnp.stack([tp.astype(jnp.int32), length])
    attended, qs, ks, vs, lse = attn_forward(scalars, dot(full_one, w_proj), cosine, sine)
    attn_branch = scatter_rows(dot_nt(attended, w_out))
    resid_one = tokens + attn_branch

    cond_kv = dot(own_context, w_kv).astype(bf16)
    cond_kv = jnp.pad(cond_kv, ((0, CROSS_KEYS - cond_count), (0, 0)))
    cond_kv = sent_to_all(cond_kv, "x", 4).reshape(4, CROSS_KEYS, 2, quarter)
    cond_kv = cond_kv.transpose(2, 1, 0, 3).reshape(2, CROSS_KEYS, local_width)
    seen = jnp.pad(own_mask > 0, (0, CROSS_KEYS - cond_count))
    bias = jnp.broadcast_to(jnp.where(seen, 0.0, masked_fill)[:, None], (CROSS_KEYS, 2 * own_rows)).astype(f32)
    norm_two, scale_two = unit_norm(resid_one)
    pair_two = pair_rows(norm_two.astype(bf16))
    cross_q = (dot(pair_two, w_cq) * HD ** (-0.5)).astype(bf16)
    cross_att = cross_forward(cross_q, cond_kv[0], cond_kv[1], bias)
    cross_branch = pair_sum(dot_nt(cross_att, w_co))
    resid_two = resid_one + cross_branch

    norm_three, scale_three = unit_norm(resid_two)
    full_three = gather_rows(norm_three.astype(bf16))
    upstream = permuted(u_own)
    full_grad = gather_rows(upstream)
    gate_up = dot(full_three, w_feed)
    gate, upward = gate_up[:, :hidden_quarter], gate_up[:, hidden_quarter:]
    sig = jax.nn.sigmoid(gate)
    hidden = (gate * sig * upward).astype(bf16)
    grad_hidden = dot(full_grad, w_down)
    grad_gate = grad_hidden * upward * sig * (1.0 + gate * (1.0 - sig))
    grad_gate_up = jnp.concatenate([grad_gate.astype(bf16), (grad_hidden * gate * sig).astype(bf16)], axis=1)
    grad_three = scatter_rows(dot_nt(grad_gate_up, w_feed))
    feed_branch = scatter_rows(dot_nt(hidden, w_down))
    output = resid_two + feed_branch
    sum_feed = scatter_plane(dot_tn(full_three, grad_gate_up).astype(bf16))
    sum_down = scatter_plane(dot_tn(full_grad, hidden).astype(bf16))
    grad_resid_two = upstream.astype(f32) + unit_norm_back(norm_three, scale_three, grad_three)

    pair_grad = pair_rows(grad_resid_two.astype(bf16))
    grad_cross_att = dot(pair_grad, w_co).astype(bf16)
    grad_cq, grad_ckv = cross_backward(cross_q, cond_kv[0], cond_kv[1], bias, grad_cross_att)
    grad_two = pair_sum(dot_nt(grad_cq, w_cq))
    grad_resid_one = grad_resid_two + unit_norm_back(norm_two, scale_two, grad_two)
    sum_cross = scatter_plane(
        jnp.concatenate([dot_tn(pair_two, grad_cq).astype(bf16), dot_tn(pair_grad, cross_att).astype(bf16)], axis=1)
    )
    ckv_parts = grad_ckv.reshape(CROSS_KEYS, 2, 4, quarter).transpose(2, 0, 1, 3).reshape(4, CROSS_KEYS, 2 * quarter)
    ckv_parts = lax.all_to_all(ckv_parts, "x", split_axis=0, concat_axis=0, tiled=True)
    ckv_share = jnp.sum(ckv_parts.astype(f32), axis=0)[:cond_count].astype(bf16)
    grad_keyval = dot_tn(own_context, ckv_share).astype(bf16)
    cond_part = dot_nt(ckv_share, w_kv)
    cond_part = (cond_part + to_partner(cond_part)).astype(bf16)
    cond_rows = -(-cond_count // 4)
    cond_part = jnp.pad(cond_part, ((0, 4 * cond_rows - cond_count), (0, 0))).reshape(4, cond_rows, D)
    cond_part = lax.all_to_all(cond_part, "x", split_axis=0, concat_axis=0, tiled=True)
    cond_own = jnp.sum(cond_part.astype(f32), axis=0).astype(bf16)
    cond_all = sent_to_all(cond_own, CTX, 8).reshape(4, 2, cond_rows, D).transpose(1, 0, 2, 3)
    cond_grad = permuted(cond_all.reshape(2, 4 * cond_rows, D)[:, :cond_count]).astype(f32)

    full_back = gather_rows(grad_resid_one.astype(bf16))
    grad_att = dot(full_back, w_out).astype(bf16)
    sum_out = scatter_plane(jnp.concatenate([grad_keyval, dot_tn(full_back, attended).astype(bf16)], axis=1))
    grad_qkv = attn_backward(qs, ks, vs, grad_att, lse, cosine, sine)
    sum_proj = scatter_plane(dot_tn(full_one, grad_qkv).astype(bf16))
    grad_one = scatter_rows(dot_nt(grad_qkv, w_proj))
    in_grad = grad_resid_one + unit_norm_back(norm_one, scale_one, grad_one)

    def placed(rows):
        moved = lax.ppermute(permuted(rows.astype(bf16)), ("yh", "tp"), SWAP)
        return lax.all_gather(moved, "tp", axis=0, tiled=False)

    layer_out = placed(output)
    in_grad = placed(in_grad).astype(f32)

    row = jnp.arange(own_rows, dtype=jnp.int32)
    valid = ((2 * x + tp) * own_rows + row < length)[:, None]
    sums = jnp.stack(
        [jnp.sum(jnp.where(valid, v * v, 0.0)) for v in (tokens, attn_branch, cross_branch, feed_branch, output)]
    )
    sums = sent_to_all(jnp.pad(sums, (0, 123))[None], ("x", "yh", "tp"), 16).reshape(4, 2, 2, 128)
    sums = jnp.sum(sums, axis=(0, 2))[:, :5]
    layer_stats = jnp.sqrt(sums / (lengths.astype(f32)[:, None] * D))

    def collected(v):
        return sent_to_all(v, CTX, 8).reshape(4, 2, half_rows, v.shape[1]).transpose(1, 2, 0, 3).reshape(2 * half_rows, 4, v.shape[1])

    cross_parts = sum_cross.reshape(half_rows, 2, 4, quarter).transpose(2, 0, 1, 3).reshape(4, half_rows, 2 * quarter)
    cross_parts = lax.all_to_all(cross_parts, "x", split_axis=0, concat_axis=0, tiled=True)
    cross_share = jnp.sum(cross_parts.astype(f32), axis=0).astype(bf16)
    feed_all = collected(jnp.concatenate([sum_feed, sum_down], axis=1)).astype(f32)
    mid_all = collected(jnp.concatenate([cross_share, sum_out[:, : 3 * quarter]], axis=1)).astype(f32)
    proj_all = collected(jnp.concatenate([sum_proj[:, k * WIDE : k * WIDE + quarter] for k in range(3)], axis=1)).astype(f32)
    feed_all = feed_all.reshape(2 * half_rows, 4, 3, hidden_quarter).transpose(0, 2, 1, 3).reshape(2 * half_rows, 3, 4 * hidden_quarter)
    mid_all = mid_all.reshape(2 * half_rows, 4, 5, quarter).transpose(0, 2, 1, 3).reshape(2 * half_rows, 5, 4 * quarter)
    proj_all = proj_all.reshape(2 * half_rows, 4, 3, quarter).transpose(0, 2, 1, 3).reshape(2 * half_rows, 3, 4 * quarter)

    def gain_of(w, raw):
        return jnp.sum(w.astype(f32) * raw, axis=tuple(range(1, raw.ndim)))

    raw_feed, raw_cq = feed_all[:, :2], mid_all[:, 0]
    gains = jnp.stack([gain_of(self_proj, proj_all), gain_of(cross_query, raw_cq), gain_of(feed_in, raw_feed)])
    gains = gains + to_partner(gains)

    def by_gain(raw, gain):
        return raw * gain.astype(f32).reshape((-1,) + (1,) * (raw.ndim - 1))

    return (
        layer_out,
        in_grad,
        cond_grad,
        layer_stats,
        gains[0],
        by_gain(proj_all, gain_attn),
        mid_all[:, 4],
        gains[1],
        by_gain(raw_cq, gain_cross),
        mid_all[:, 2:4],
        mid_all[:, 1],
        gains[2],
        by_gain(raw_feed, gain_feed),
        feed_all[:, 2],
    )


def solution(mesh):
    fine = Mesh(mesh.devices.reshape(4, 2, 4, 2, 2), ("z", "yl", "x", "yh", "tp"))
    weights = (
        P(DP),
        P(DP, None, "tp"),
        P(DP, "tp"),
        P(DP),
        P(DP, "tp"),
        P(DP, None, "tp"),
        P(DP, "tp"),
        P(DP),
        P(DP, None, "tp"),
        P(DP, "tp"),
    )
    return jax.shard_map(
        per_device,
        mesh=fine,
        in_specs=(P(DP, CTX, None), P(DP, None, None), P(DP), P(DP, None), P(DP, CTX, None), *weights),
        out_specs=(P(DP, CTX, None), P(DP, CTX, None), P(DP, None, None), P(DP, None), *weights),
        check_vma=False,
    )
```

```python
import jax
import jax.numpy as jnp
from jax import lax
from jax.experimental import pallas as pl
from jax.experimental.pallas import tpu as pltpu
from jax.sharding import Mesh
from jax.sharding import PartitionSpec as P

DP = ("z", "yl")
CTX = ("x", "yh")
PLANE = ("z", "yh", "yl")
SWAP = ((0, 0), (1, 2), (2, 1), (3, 3))

D = 1536
HD = 64
ROT = 32
HEADS = 3
WIDE = 256
V_AT, K_AT, O_AT, QVK = 128, 384, 512, 640
ROWS = 128
SEQ = 1024
QB = 256
CROSS_KEYS = 144
norm_eps = 1e-05
masked_fill = -1e30
bf16 = jnp.bfloat16
f32 = jnp.float32


def permuted(v):
    parts = []
    for z in range(v.shape[-1] // 384):
        for piece in (0, 2, 1, 3):
            at = z * 384 + piece * 96
            parts.append(v[..., at : at + 96])
    return jnp.concatenate(parts, axis=-1)


def dot(a, b):
    return jnp.dot(a, b, preferred_element_type=f32)


def dot_nt(a, b):
    return lax.dot_general(a, b, (((1,), (1,)), ((), ())), preferred_element_type=f32)


def dot_tn(a, b):
    return lax.dot_general(a, b, (((0,), (0,)), ((), ())), preferred_element_type=f32)


def to_partner(v):
    return lax.ppermute(v, "tp", ((0, 1), (1, 0)))


def exchanged(v, axes):
    return lax.all_to_all(v, axes, split_axis=0, concat_axis=0, tiled=True)


def sent_to_all(v, axes, count):
    return exchanged(jnp.broadcast_to(v[None], (count, *v.shape)), axes)


def after(values, *others):
    return lax.optimization_barrier((values, others))[0]


def both(first, *others):
    return lax.optimization_barrier((first, *others))


def along_x(v, step):
    return lax.ppermute(v, "x", [(i, (i + step) % 4) for i in range(4)])


def gather_x(own):
    return [own] + [along_x(own, step) for step in (1, 2, 3)]


def scatter_x(blocks):
    return [blocks[0]] + [along_x(blocks[step], -step) for step in (1, 2, 3)]


def swapped_x(blocks):
    return [blocks[0]] + [along_x(blocks[step], step) for step in (1, 2, 3)]


def summed(blocks):
    return sum(block.astype(f32) for block in blocks[1:]) + blocks[0].astype(f32)


def gather_half(own):
    return jnp.concatenate(gather_x(own), axis=0)


def to_far(v):
    return lax.ppermute(v, "yh", ((0, 1), (1, 0)))


def with_partner(mine):
    return jnp.concatenate([mine, to_partner(mine)], axis=0)


def scatter_half(partial):
    half = 4 * ROWS
    got = to_partner(partial[half:].astype(bf16))
    mine = (partial[:half].astype(f32) + got.astype(f32)).astype(bf16)
    return [mine[k * ROWS : (k + 1) * ROWS] for k in range(4)]


def plane_parts(grad):
    return exchanged(grad.astype(bf16).reshape(16, grad.shape[0] // 16, grad.shape[1]), PLANE)


def total(parts):
    return jnp.sum(parts.astype(f32), axis=0)


def pair_rows(own):
    return jnp.concatenate([own, to_partner(own)], axis=0)


def pair_sum(partial):
    return partial[:ROWS] + to_partner(partial[ROWS:])


def gather_plane(shard):
    return lax.all_gather(shard, PLANE, axis=0, tiled=True)


def scatter_plane(grad):
    return lax.psum_scatter(grad, PLANE, scatter_dimension=0, tiled=True)


def unit_norm(v):
    centered = v - jnp.mean(v, axis=-1, keepdims=True)
    scale = lax.rsqrt(jnp.mean(centered * centered, axis=-1, keepdims=True) + norm_eps)
    return centered * scale, scale


def unit_norm_back(x_hat, scale, grad):
    along = jnp.mean(grad * x_hat, axis=-1, keepdims=True)
    return scale * (grad - jnp.mean(grad, axis=-1, keepdims=True) - x_hat * along)


def lane_masks(rows):
    lane = lax.broadcasted_iota(jnp.int32, (rows, WIDE), 1)
    heads = [(lane // HD == h).astype(f32).astype(bf16) for h in range(HEADS + 1)]
    return lane, heads, (lane == HEADS * HD).astype(f32).astype(bf16)


def turned(v, cosine, sine, first):
    other = jnp.where(first, pltpu.roll(v, WIDE - ROT // 2, 1), pltpu.roll(v, ROT // 2, 1))
    cosine, sine = (jnp.concatenate([table, table], axis=1) for table in (cosine, sine))
    return v * cosine, other * sine


def attn_forward_kernel(sc, qkv, cosine, sine, att, qs, ks, vs, lse, vt):
    lane, heads, extra = lane_masks(QB)
    first = lane % HD < ROT // 2
    value_head = lax.broadcasted_iota(jnp.int32, (WIDE, QB), 0) // HD - 1

    def prepare(block, carry):
        rows = pl.ds(block * QB, QB)
        c, s = cosine[rows, :], sine[rows, :]
        straight, crossed = turned(qkv[rows, 0:WIDE], c, s, first)
        query = ((straight + crossed) * HD ** (-0.5)).astype(bf16)
        qs[rows, :] = jnp.where(lane < HEADS * HD, query.astype(f32), jnp.where(lane == HEADS * HD, 1.0, 0.0)).astype(bf16)
        straight, crossed = turned(qkv[rows, K_AT : K_AT + WIDE], c, s, first)
        row = lax.broadcasted_iota(jnp.int32, (QB, WIDE), 0) + block * QB
        side = jnp.where(row < SEQ // 2, sc[0], 1 - sc[0])
        within = row % (SEQ // 2)
        place = ((sc[2] + 4 - within // ROWS) % 4 * 2 + side) * ROWS + within % ROWS
        fill = jnp.where((lane == HEADS * HD) & (place >= sc[1]), masked_fill, 0.0)
        ks[rows, :] = jnp.where(lane < HEADS * HD, straight + crossed, fill).astype(bf16)
        value = qkv[rows, V_AT : V_AT + WIDE]
        vs[rows, :] = value.astype(bf16)
        vt[:, rows] = value.T.astype(bf16)
        return carry

    for block in range(SEQ // QB):
        prepare(block, 0)

    def attend(block, carry):
        rows = pl.ds(pl.multiple_of(block * QB, QB), QB)
        query = qs[rows, :]
        total = jnp.zeros((WIDE, QB), f32)
        for h in range(HEADS):
            scores = dot_nt(ks[...], query * (heads[h] + extra))
            top = jnp.max(scores, axis=0, keepdims=True)
            weight = jnp.exp(scores - top)
            mass = jnp.sum(weight, axis=0, keepdims=True)
            out = dot(vt[...], weight.astype(bf16))
            total = jnp.where(value_head == h, out / mass, total)
            lse[h : h + 1, rows] = top + jnp.log(mass)
        att[rows, :] = total.T.astype(bf16)
        return carry

    lse[...] = jnp.zeros(lse.shape, f32)
    lax.fori_loop(0, SEQ // QB, attend, 0)


def attn_forward(scalars, qkv, cosine, sine):
    wide = jax.ShapeDtypeStruct((SEQ, WIDE), bf16)
    return pl.pallas_call(
        attn_forward_kernel,
        in_specs=[pl.BlockSpec(memory_space=pltpu.SMEM)] + [pl.BlockSpec(memory_space=pltpu.VMEM)] * 3,
        out_shape=(wide, wide, wide, wide, jax.ShapeDtypeStruct((8, SEQ), f32)),
        scratch_shapes=[pltpu.VMEM((WIDE, SEQ), bf16)],
        cost_estimate=pl.CostEstimate(flops=4 * HEADS * SEQ * SEQ * WIDE, transcendentals=HEADS * SEQ * SEQ, bytes_accessed=8 << 20),
    )(scalars, qkv, cosine, sine)


def attn_backward_kernel(qs, ks, vs, grad, lse, cosine, sine, out, kt, dq, dk, dv):
    lane, heads, extra = lane_masks(QB)
    first = lane % HD < ROT // 2
    wide_head = lax.broadcasted_iota(jnp.int32, (WIDE, QB), 0) // HD
    kept = lane < HEADS * HD
    kt[...] = ks[...].astype(f32).T.astype(bf16)
    dk[...] = jnp.zeros(dk.shape, f32)
    dv[...] = jnp.zeros(dv.shape, f32)

    def step(block, carry):
        rows = pl.ds(pl.multiple_of(block * QB, QB), QB)
        query, given = qs[rows, :], grad[rows, :]
        total = jnp.zeros((WIDE, QB), f32)
        for h in range(HEADS):
            own_query, own_grad = query * heads[h], given * heads[h + 1]
            scores = dot_nt(ks[...], query * (heads[h] + extra))
            weight = jnp.exp(scores - lse[h : h + 1, rows])
            wanted = dot_nt(vs[...], own_grad)
            product = weight * wanted
            inner = jnp.sum(product, axis=0, keepdims=True)
            slope = (product - weight * inner).astype(bf16)
            dv[...] += dot(weight.astype(bf16), own_grad)
            dk[...] += dot(slope, own_query)
            total = jnp.where(wide_head == h, dot(kt[...], slope), total)
        straight, crossed = turned(total.T * HD ** (-0.5), cosine[rows, :], sine[rows, :], first)
        turned_back = straight - crossed
        out[rows, 0:128] = turned_back[:, :128].astype(bf16)
        dq[rows, :] = turned_back[:, 128:]
        return carry

    lax.fori_loop(0, SEQ // QB, step, 0)
    for block in range(SEQ // QB):
        rows = pl.ds(block * QB, QB)
        value = dv[rows, :]
        out[rows, V_AT : V_AT + 128] = jnp.where(lane[:, :128] < HD, dq[rows, :], value[:, :128]).astype(bf16)
        out[rows, V_AT + 128 : V_AT + 256] = value[:, 128:].astype(bf16)
        straight, crossed = turned(dk[rows, :], cosine[rows, :], sine[rows, :], first)
        out[rows, K_AT : K_AT + WIDE] = jnp.where(kept, straight - crossed, 0.0).astype(bf16)


def attn_backward(qs, ks, vs, grad, lse, cosine, sine):
    return pl.pallas_call(
        attn_backward_kernel,
        in_specs=[pl.BlockSpec(memory_space=pltpu.VMEM)] * 7,
        out_shape=jax.ShapeDtypeStruct((SEQ, QVK), bf16),
        scratch_shapes=[pltpu.VMEM((WIDE, SEQ), bf16), pltpu.VMEM((SEQ, 128), f32), pltpu.VMEM((SEQ, WIDE), f32), pltpu.VMEM((SEQ, WIDE), f32)],
        cost_estimate=pl.CostEstimate(flops=10 * HEADS * SEQ * SEQ * WIDE, transcendentals=HEADS * SEQ * SEQ, bytes_accessed=8 << 20),
    )(qs, ks, vs, grad, lse, cosine, sine)


PAIR = 2 * HD
QUARTER = HEADS * HD


def pair_of(sc, kv, group, kind):
    lanes = []
    for head in (2 * group, 2 * group + 1):
        at = kind * QUARTER + head % HEADS * HD
        lanes.append(kv[(sc[2] + 4 - head // HEADS) % 4, :, at : at + HD])
    return jnp.concatenate(lanes, axis=1)


def cross_weights(query, keys, bias):
    scores = dot_nt(keys, query) + bias
    weight = jnp.exp(scores - jnp.max(scores, axis=0, keepdims=True))
    return weight / jnp.sum(weight, axis=0, keepdims=True)


def store_quarters(sc, out, group, value):
    for h in range(2):
        head = 2 * group + h
        at = head % HEADS * HD
        for side in range(2):
            piece = value[side * ROWS : (side + 1) * ROWS, h * HD : (h + 1) * HD]
            out[(head // HEADS + 4 - sc[2]) % 4, 0:ROWS, side * QUARTER + at : side * QUARTER + at + HD] = piece


def cross_forward_kernel(sc, cq, kv, bias, att, quarters):
    lane = lax.broadcasted_iota(jnp.int32, (2 * ROWS, PAIR), 1)
    row = lax.broadcasted_iota(jnp.int32, (PAIR, 2 * ROWS), 0)
    for group in range(cq.shape[1] // PAIR):
        at = pl.ds(group * PAIR, PAIR)
        query, keys = cq[:, at], pair_of(sc, kv, group, 0)
        values = pair_of(sc, kv, group, 1).astype(f32).T.astype(bf16)
        outs = []
        for h in range(2):
            mask = (lane // HD == h).astype(f32).astype(bf16)
            weight = cross_weights(query * mask, keys, bias[...])
            outs.append(dot(values, weight.astype(bf16)))
        value = jnp.where(row < HD, outs[0], outs[1]).T.astype(bf16)
        att[:, at] = value
        store_quarters(sc, quarters, group, value)


def cross_forward(scalars, cq, kv, bias):
    return pl.pallas_call(
        cross_forward_kernel,
        in_specs=[pl.BlockSpec(memory_space=pltpu.SMEM)] + [pl.BlockSpec(memory_space=pltpu.VMEM)] * 3,
        out_shape=(jax.ShapeDtypeStruct(cq.shape, bf16), jax.ShapeDtypeStruct((4, ROWS, 2 * QUARTER), bf16)),
        cost_estimate=pl.CostEstimate(flops=4 * 12 * 256 * 144 * 128, transcendentals=12 * 256 * 144, bytes_accessed=2 << 20),
    )(scalars, cq, kv, bias)


def cross_backward_kernel(sc, cq, kv, bias, grad, dq, quarters):
    lane = lax.broadcasted_iota(jnp.int32, (2 * ROWS, PAIR), 1)
    row = lax.broadcasted_iota(jnp.int32, (PAIR, 2 * ROWS), 0)
    for group in range(cq.shape[1] // PAIR):
        at = pl.ds(group * PAIR, PAIR)
        query, given = cq[:, at], grad[:, at]
        keys, values = pair_of(sc, kv, group, 0), pair_of(sc, kv, group, 1)
        turned_keys = keys.astype(f32).T.astype(bf16)
        outs, grads = [], [0.0, 0.0]
        for h in range(2):
            mask = (lane // HD == h).astype(f32).astype(bf16)
            own_query, own_grad = query * mask, given * mask
            weight = cross_weights(own_query, keys, bias[...])
            product = weight * dot_nt(values, own_grad)
            slope = (product - weight * jnp.sum(product, axis=0, keepdims=True)).astype(bf16)
            outs.append(dot(turned_keys, slope))
            grads[0] += dot(slope, own_query)
            grads[1] += dot(weight.astype(bf16), own_grad)
        value = (jnp.where(row < HD, outs[0], outs[1]).T * HD ** (-0.5)).astype(bf16)
        dq[:, at] = value
        store_quarters(sc, quarters, group, value)
        for h in range(2):
            head = 2 * group + h
            for kind in range(2):
                place = kind * QUARTER + head % HEADS * HD
                piece = grads[kind][:, h * HD : (h + 1) * HD].astype(bf16)
                quarters[(head // HEADS + 4 - sc[2]) % 4, ROWS:, place : place + HD] = piece


def cross_backward(scalars, cq, kv, bias, grad):
    return pl.pallas_call(
        cross_backward_kernel,
        in_specs=[pl.BlockSpec(memory_space=pltpu.SMEM)] + [pl.BlockSpec(memory_space=pltpu.VMEM)] * 4,
        out_shape=(
            jax.ShapeDtypeStruct(cq.shape, bf16),
            jax.ShapeDtypeStruct((4, ROWS + kv.shape[1], 2 * QUARTER), bf16),
        ),
        cost_estimate=pl.CostEstimate(flops=10 * 12 * 256 * 144 * 128, transcendentals=12 * 256 * 144, bytes_accessed=3 << 20),
    )(scalars, cq, kv, bias, grad)


def rotary_lanes(side, x):
    row = jnp.arange(SEQ, dtype=jnp.int32)
    within = row % (SEQ // 2)
    part = jnp.where(row < SEQ // 2, side, 1 - side)
    place = (((x + 4 - within // ROWS) % 4 * 2 + part) * ROWS + within % ROWS).astype(f32)
    lane = jnp.arange(128, dtype=jnp.int32) % HD
    exponent = (lane % (ROT // 2)).astype(f32) * (2.0 / ROT)
    angle = place[:, None] * jnp.power(jnp.float32(10000.0), -exponent)[None, :]
    inside = (lane < ROT)[None, :]
    sign = jnp.where(lane < ROT // 2, -1.0, 1.0)[None, :]
    return jnp.where(inside, jnp.cos(angle), 1.0), jnp.where(inside, jnp.sin(angle) * sign, 0.0)


def products_kernel(count, *refs):
    out, at = refs[-1], 0
    for k in range(count):
        left, right = refs[2 * k], refs[2 * k + 1]
        width = right.shape[1]
        out[:, at : at + width] = dot_tn(left[...], right[...]).astype(bf16)
        at += width


def products(*pairs):
    tile, total_width = 256, sum(right.shape[1] for _, right in pairs)
    flat, specs = [], []
    for left, right in pairs:
        flat += [left, right]
        specs += [pl.BlockSpec((left.shape[0], tile), lambda i: (0, i)), pl.BlockSpec(right.shape, lambda i: (0, 0))]
    work = sum(left.shape[0] * right.shape[1] for left, right in pairs)
    return pl.pallas_call(
        lambda *refs: products_kernel(len(pairs), *refs),
        grid=(D // tile,),
        in_specs=specs,
        out_specs=pl.BlockSpec((tile, total_width), lambda i: (i, 0)),
        out_shape=jax.ShapeDtypeStruct((D, total_width), bf16),
        cost_estimate=pl.CostEstimate(flops=2 * D * work, transcendentals=0, bytes_accessed=10 << 20),
    )(*flat)


def by_rows(blocks):
    return jnp.concatenate([b[:ROWS, k * QUARTER : (k + 1) * QUARTER] for k in range(2) for b in blocks], axis=0)


def attn_products_kernel(one, grad, back, att, context, share, two, three, *rest):
    cq, catt, out = rest[:4], rest[4:8], rest[8]
    proj, across = dot_tn(one[...], grad[...]), dot_tn(back[...], att[...])
    out[:, :O_AT] = proj[:, :O_AT].astype(bf16)
    out[:, O_AT:QVK] = (proj[:, O_AT:] + across[:, : QVK - O_AT]).astype(bf16)
    out[:, QVK : O_AT + WIDE] = across[:, QVK - O_AT :].astype(bf16)
    at = O_AT + WIDE
    out[:, at : at + 2 * QUARTER] = dot_tn(context[...], share[...]).astype(bf16)
    at += 2 * QUARTER
    pieces = [dot_tn(left[...], by_rows(right)).astype(bf16) for left, right in ((two, cq), (three, catt))]
    out[:, at:] = jnp.concatenate(pieces, axis=1)


def attn_products(one, grad, back, att, context, share, two, three, cq, catt):
    tile, width = 256, O_AT + WIDE + 4 * QUARTER

    def whole(v):
        return pl.BlockSpec(v.shape, lambda i: (0, 0))

    def piece(v):
        return pl.BlockSpec((v.shape[0], tile), lambda i: (0, i))

    specs = [piece(one), whole(grad), piece(back), whole(att), piece(context), whole(share), piece(two), piece(three)]
    return pl.pallas_call(
        attn_products_kernel,
        grid=(D // tile,),
        in_specs=specs + [whole(v) for v in (*cq, *catt)],
        out_specs=pl.BlockSpec((tile, width), lambda i: (i, 0)),
        out_shape=jax.ShapeDtypeStruct((D, width), bf16),
        cost_estimate=pl.CostEstimate(flops=2 * D * SEQ * width, transcendentals=0, bytes_accessed=16 << 20),
    )(one, grad, back, att, context, share, two, three, *cq, *catt)


def finish_feed_kernel(at, parts, gain, grad_in, grad_down):
    width = grad_down.shape[1]
    for kind in range(2):
        grad_in[kind] = parts[0, :, kind * width : (kind + 1) * width].astype(f32) * gain[...]
    grad_down[...] = parts[0, :, 2 * width :].astype(f32)


def held_at(h, q, at):
    return (at[0] + 4 - q) % 4 * 2 + jnp.where(h == at[1], 0, 1)


def finish_feed(at, parts, gain):
    rows, width = parts.shape[1], parts.shape[2] // 3
    return pl.pallas_call(
        finish_feed_kernel,
        grid_spec=pltpu.PrefetchScalarGridSpec(
            num_scalar_prefetch=1,
            grid=(2, 4),
            in_specs=[
                pl.BlockSpec((1, rows, 3 * width), lambda h, q, at: (held_at(h, q, at), 0, 0)),
                pl.BlockSpec((rows, 1), lambda h, q, at: (h, 0)),
            ],
            out_specs=(
                pl.BlockSpec((2, rows, width), lambda h, q, at: (0, h, q)),
                pl.BlockSpec((rows, width), lambda h, q, at: (h, q)),
            ),
        ),
        out_shape=(
            jax.ShapeDtypeStruct((2, 2 * rows, 4 * width), f32),
            jax.ShapeDtypeStruct((2 * rows, 4 * width), f32),
        ),
        cost_estimate=pl.CostEstimate(flops=1 << 22, transcendentals=0, bytes_accessed=11 << 20),
    )(at, parts, gain)


def finish_cond_kernel(at, parts, out):
    width = parts.shape[2]
    for h in range(2):
        for q in range(4):
            out[h, :, q * width : (q + 1) * width] = parts[held_at(h, q, at)].astype(f32)


def finish_cond(at, parts):
    count, width = parts.shape[1:]
    return pl.pallas_call(
        finish_cond_kernel,
        in_specs=[pl.BlockSpec(memory_space=pltpu.SMEM), pl.BlockSpec(memory_space=pltpu.VMEM)],
        out_shape=jax.ShapeDtypeStruct((2, count, 4 * width), f32),
        cost_estimate=pl.CostEstimate(flops=1 << 20, transcendentals=0, bytes_accessed=3 << 20),
    )(at, parts)


def finish_columns(places, parts, gain, other_gain):
    rows, quarter = parts.shape[1], parts.shape[2] // 8
    width = 4 * quarter

    def kernel(places, parts, gain, other_gain, proj, out, keyval, query, cross):
        h = pl.program_id(0)

        def kind_of(kind):
            row = [parts[places[4 * h + q], :, kind * quarter : (kind + 1) * quarter].astype(f32) for q in range(4)]
            return jnp.concatenate(row, axis=1)

        for place, kind in enumerate((0, 2, 1)):
            proj[place] = kind_of(kind) * gain[...]
        out[...] = kind_of(3)
        keyval[0] = kind_of(4)
        keyval[1] = kind_of(5)
        query[...] = kind_of(6) * other_gain[...]
        cross[...] = kind_of(7)

    def stacked(count):
        return pl.BlockSpec((count, rows, width), lambda h, places: (0, h, 0)), jax.ShapeDtypeStruct((count, 2 * rows, width), f32)

    plain = pl.BlockSpec((rows, width), lambda h, places: (h, 0)), jax.ShapeDtypeStruct((2 * rows, width), f32)
    outs = [stacked(3), plain, stacked(2), plain, plain]
    return pl.pallas_call(
        kernel,
        grid_spec=pltpu.PrefetchScalarGridSpec(
            num_scalar_prefetch=1,
            grid=(2,),
            in_specs=[
                pl.BlockSpec(parts.shape, lambda h, places: (0, 0, 0)),
                pl.BlockSpec((rows, 1), lambda h, places: (h, 0)),
                pl.BlockSpec((rows, 1), lambda h, places: (h, 0)),
            ],
            out_specs=[spec for spec, _ in outs],
        ),
        out_shape=[shape for _, shape in outs],
        cost_estimate=pl.CostEstimate(flops=1 << 20, transcendentals=0, bytes_accessed=4 << 20),
    )(places, parts, gain, other_gain)


def per_device(
    hidden_in,
    context,
    lengths,
    cond_mask,
    out_grad,
    gain_attn,
    self_proj,
    self_out,
    gain_cross,
    cross_query,
    cross_keyval,
    cross_out,
    gain_feed,
    feed_in,
    feed_out,
):
    x, yh, tp = lax.axis_index("x"), lax.axis_index("yh"), lax.axis_index("tp")
    cond_count = context.shape[1]
    own_rows = hidden_in.shape[1]
    half_rows = self_proj.shape[0] // 2
    quarter = self_proj.shape[2] // 4
    hidden_quarter = feed_in.shape[2] // 4
    local_width = self_proj.shape[2]

    def own_half(w):
        return lax.dynamic_slice_in_dim(w, yh * half_rows, half_rows, 0)

    def own_cols(w, count):
        return lax.dynamic_slice_in_dim(w, x * count, count, w.ndim - 1)

    def scaled(w, gain):
        return (w.astype(f32) * own_half(gain).astype(f32)[:, None]).astype(bf16)

    x_own = lax.ppermute(lax.dynamic_index_in_dim(hidden_in, tp, 0, False), ("yh", "tp"), SWAP)
    u_own = lax.ppermute(lax.dynamic_index_in_dim(out_grad, tp, 0, False), ("yh", "tp"), SWAP)
    length = lax.dynamic_index_in_dim(lengths, yh, 0, False)
    own_mask = lax.dynamic_index_in_dim(cond_mask, yh, 0, False)
    tokens = permuted(x_own).astype(f32)
    norm_one, scale_one = unit_norm(tokens)

    qkv_cols = own_cols(own_half(self_proj), quarter)
    qvk_cols = jnp.concatenate([qkv_cols[:, 0], qkv_cols[:, 2], qkv_cols[:, 1]], axis=1)
    out_cols = own_cols(own_half(self_out), quarter)
    keyval_cols = own_cols(own_half(cross_keyval), quarter).reshape(half_rows, 2 * quarter)
    cq_half = own_half(cross_query)
    first_set = gather_plane(
        jnp.concatenate([scaled(qvk_cols, gain_attn), out_cols, keyval_cols, scaled(cq_half, gain_cross), own_half(cross_out)], axis=1)
    )
    sent_one = norm_one.astype(bf16)
    sent_one, feed_in, feed_out, context = both(sent_one, feed_in, feed_out, context)
    feed_cols = own_cols(own_half(feed_in), hidden_quarter).reshape(half_rows, 2 * hidden_quarter)
    down_cols = own_cols(own_half(feed_out), hidden_quarter)
    feed_set = gather_plane(jnp.concatenate([scaled(feed_cols, gain_feed), down_cols], axis=1))
    w_qvk, w_out = first_set[:, :QVK], first_set[:, O_AT : O_AT + WIDE]
    cq_at = O_AT + WIDE + 2 * quarter
    w_kv, w_cq, w_co = first_set[:, O_AT + WIDE : cq_at], first_set[:, cq_at : cq_at + local_width], first_set[:, cq_at + local_width :]
    w_feed, w_down = feed_set[:, : 2 * hidden_quarter], feed_set[:, 2 * hidden_quarter :]

    scalars = jnp.stack([tp.astype(jnp.int32), length, x.astype(jnp.int32)])
    own_context = jnp.pad(lax.dynamic_index_in_dim(context, yh, 0, False), ((0, CROSS_KEYS - cond_count), (0, 0)))
    mine_one, u_own, cosine, sine, own_context = both(
        gather_half(sent_one), u_own, *rotary_lanes(tp, x), permuted(own_context)
    )
    upstream = permuted(u_own)
    full_one, mine_grad = both(with_partner(mine_one), gather_half(upstream))
    qvk, keyval, full_grad = both(dot(full_one, w_qvk), dot(own_context, w_kv).astype(bf16), with_partner(mine_grad))
    attended, qs, ks, vs, lse = attn_forward(scalars, qvk, cosine, sine)
    attended, keyval = both(attended, gather_x(keyval))
    cond_kv = jnp.stack(keyval)
    blocks = both(*scatter_half(dot_nt(attended, w_out)))
    attn_branch = summed(both(*scatter_x(blocks)))
    resid_one = tokens + attn_branch

    seen = jnp.pad(own_mask > 0, (0, CROSS_KEYS - cond_count))
    bias = jnp.broadcast_to(jnp.where(seen, 0.0, masked_fill)[:, None], (CROSS_KEYS, 2 * own_rows)).astype(f32)
    norm_two, scale_two = unit_norm(resid_one)
    sent_two = norm_two.astype(bf16)
    pair_two = pair_rows(sent_two)
    cross_q = (dot(pair_two, w_cq) * HD ** (-0.5)).astype(bf16)
    cross_att, att_quarters = cross_forward(scalars, cross_q, cond_kv, bias)
    cross_branch = pair_sum(dot_nt(cross_att, w_co))
    resid_two = resid_one + cross_branch
    norm_three, scale_three = unit_norm(resid_two)

    sent_three, full_grad, sent_two, att_quarters = both(norm_three.astype(bf16), full_grad, sent_two, att_quarters)
    mine_three, grad_hidden = both(gather_half(sent_three), dot(full_grad, w_down))
    full_three, sent_two, att_quarters = both(with_partner(mine_three), sent_two, att_quarters)
    carried = [jnp.concatenate([sent_two, att_quarters[k]], axis=1) for k in range(4)]
    carried = swapped_x(carried)
    gate_up = dot(full_three, w_feed)
    gate, upward = gate_up[:, :hidden_quarter], gate_up[:, hidden_quarter:]
    sig = jax.nn.sigmoid(gate)
    hidden = (gate * sig * upward).astype(bf16)
    grad_gate = grad_hidden * upward * sig * (1.0 + gate * (1.0 - sig))
    grad_gate_up = jnp.concatenate([grad_gate.astype(bf16), (grad_hidden * gate * sig).astype(bf16)], axis=1)
    partial, carried = both(dot_nt(grad_gate_up, w_feed), carried)
    blocks, carried, grad_gate_up, hidden = both(scatter_half(partial), carried, grad_gate_up, hidden)
    mine_two = jnp.concatenate([block[:, :D] for block in carried], axis=0)
    att_quarter = carried
    grad_three, grad_feed, feed_part, full_two = both(
        scatter_x(blocks),
        products((full_three, grad_gate_up), (full_grad, hidden)),
        dot_nt(hidden, w_down).astype(bf16),
        with_partner(mine_two),
    )
    sum_feed = scatter_plane(grad_feed)
    grad_resid_two = upstream.astype(f32) + unit_norm_back(norm_three, scale_three, summed(grad_three))

    sent_two, feed_part = both(grad_resid_two.astype(bf16), feed_part)
    mine_two = gather_half(sent_two)
    pair_grad = pair_rows(sent_two)
    grad_cross_att = dot(pair_grad, w_co).astype(bf16)
    grad_cq, quarters = cross_backward(scalars, cross_q, cond_kv, bias, grad_cross_att)
    grad_cq, mine_two, feed_part = both(grad_cq, mine_two, feed_part)
    grad_two = pair_sum(dot_nt(grad_cq, w_cq))
    grad_resid_one = grad_resid_two + unit_norm_back(norm_two, scale_two, grad_two)

    sent_back, mine_two, quarters, feed_part, att_quarter = both(
        grad_resid_one.astype(bf16), mine_two, quarters, feed_part, att_quarter
    )
    mine_back, grad_two_all, feed_half, att_quarter = both(
        gather_half(sent_back), with_partner(mine_two), scatter_half(feed_part), [block[:, D:] for block in att_quarter]
    )
    full_back, quarters, feed_half = both(with_partner(mine_back), quarters, feed_half)
    grad_att, quarters, feed_half = both(dot(full_back, w_out).astype(bf16), quarters, feed_half)
    quarter_parts = swapped_x([quarters[k] for k in range(4)])
    feed_parts = scatter_x(feed_half)
    grad_qvk = attn_backward(qs, ks, vs, grad_att, lse, cosine, sine)
    grad_qvk, quarter_parts, sum_feed = both(grad_qvk, quarter_parts, sum_feed)
    ckv_share = summed([part[ROWS:] for part in quarter_parts]).astype(bf16)
    grad_attn = attn_products(
        full_one, grad_qvk, full_back, attended, own_context, ckv_share, full_two, grad_two_all, quarter_parts, att_quarter
    )
    grad_attn, grad_qvk, ckv_share, feed_parts, sum_feed_far = both(grad_attn, grad_qvk, ckv_share, feed_parts, to_far(sum_feed))
    parts_attn = plane_parts(grad_attn)
    blocks, ckv_share, feed_parts = both(scatter_half(dot_nt(grad_qvk, w_qvk)), ckv_share, feed_parts)
    cond_part = dot_nt(ckv_share, w_kv)[:cond_count]
    cond_part = (cond_part + to_partner(cond_part)).astype(bf16)
    feed_branch = summed(feed_parts)
    output = resid_two + feed_branch
    grad_one, cond_part, sent_out, sum_feed, sum_feed_far = both(
        scatter_x(blocks), cond_part, permuted(output.astype(bf16)), sum_feed, sum_feed_far
    )
    in_grad = grad_resid_one + unit_norm_back(norm_one, scale_one, summed(grad_one))

    def columns_of(back):
        return lax.dynamic_slice_in_dim(cond_part, (x + 4 - back) % 4 * (D // 4), D // 4, 1)

    cond_parts = scatter_x([columns_of(back) for back in range(4)])
    cond_own = permuted(summed(cond_parts).astype(bf16))
    feed_all = gather_x(jnp.stack([sum_feed, sum_feed_far]))

    def row_sums(w, grad):
        sums = jnp.sum(w.astype(f32) * grad.astype(f32), axis=1)
        return jnp.pad(sums, (0, 128 - half_rows))

    row = jnp.arange(own_rows, dtype=jnp.int32)
    valid = ((2 * x + tp) * own_rows + row < length)[:, None]
    squares = [jnp.sum(jnp.where(valid, v * v, 0.0)) for v in (tokens, attn_branch, cross_branch, feed_branch, output)]
    small = jnp.concatenate([row_sums(feed_cols, sum_feed[:, : 2 * hidden_quarter]), jnp.pad(jnp.stack(squares), (0, 123))])

    moved_in = lax.ppermute(permuted(in_grad.astype(bf16)), ("yh", "tp"), SWAP)
    moved_out = lax.ppermute(sent_out, ("yh", "tp"), SWAP)
    parts_attn, moved_in, moved_out, feed_all, small, cond_own = both(parts_attn, moved_in, moved_out, feed_all, small, cond_own)
    sum_attn = total(parts_attn)
    attn_own = sum_attn.astype(bf16)
    attn_far, cond_far = both(to_far(attn_own), to_far(cond_own))
    attn_all = gather_x(jnp.stack([attn_own, attn_far]))
    cond_all = gather_x(jnp.stack([cond_own, cond_far]))
    more = [row_sums(qvk_cols, sum_attn[:, : 3 * quarter])]
    more += [row_sums(own_cols(cq_half, quarter), sum_attn[:, 6 * quarter : 7 * quarter])]
    small = jnp.concatenate([*more, small]).reshape(4, 128)
    small_blocks = gather_x(small + to_partner(small))
    in_grad = lax.all_gather(moved_in, "tp", axis=0, tiled=False).astype(f32)
    layer_out = lax.all_gather(moved_out, "tp", axis=0, tiled=False)
    at = jnp.stack([x, yh]).astype(jnp.int32)

    def laid(blocks):
        stacked = jnp.stack(blocks)
        return stacked.reshape(8, *stacked.shape[2:])

    def column(gain):
        return gain.astype(f32)[:, None]

    grad_feed_in, grad_feed_out = finish_feed(at, laid(feed_all), column(gain_feed))
    grad_feed_in = grad_feed_in.transpose(1, 0, 2)
    attn_all, small_blocks, cond_all, grad_feed_in, grad_feed_out, in_grad, layer_out = both(
        attn_all, small_blocks, cond_all, grad_feed_in, grad_feed_out, in_grad, layer_out
    )
    cond_grad = finish_cond(at, laid(cond_all))

    block = jnp.arange(8, dtype=jnp.int32)
    places = (x + 4 - block % 4) % 4 * 2 + jnp.where(block // 4 == yh, 0, 1)
    proj, out, keyval, query, cross = finish_columns(places, laid(attn_all), column(gain_attn), column(gain_cross))
    small = jnp.stack(small_blocks)
    small = sum(lax.dynamic_index_in_dim(small, (x + 4 - q) % 4, 0, False) for q in range(4))
    other = lax.ppermute(small, "yh", ((0, 1), (1, 0)))
    small = jnp.where(yh == 0, jnp.stack([small, other]), jnp.stack([other, small]))
    layer_stats = jnp.sqrt(small[:, 3, :5] / (lengths.astype(f32)[:, None] * D))
    gains = [small[:, k, :half_rows].reshape(2 * half_rows) for k in range(3)]

    return (
        layer_out,
        in_grad,
        cond_grad,
        layer_stats,
        gains[0],
        proj.transpose(1, 0, 2),
        out,
        gains[1],
        query,
        keyval.transpose(1, 0, 2),
        cross,
        gains[2],
        grad_feed_in,
        grad_feed_out,
    )


def solution(mesh):
    fine = Mesh(mesh.devices.reshape(4, 2, 4, 2, 2), ("z", "yl", "x", "yh", "tp"))
    weights = (
        P(DP),
        P(DP, None, "tp"),
        P(DP, "tp"),
        P(DP),
        P(DP, "tp"),
        P(DP, None, "tp"),
        P(DP, "tp"),
        P(DP),
        P(DP, None, "tp"),
        P(DP, "tp"),
    )
    return jax.shard_map(
        per_device,
        mesh=fine,
        in_specs=(P(DP, CTX, None), P(DP, None, None), P(DP), P(DP, None), P(DP, CTX, None), *weights),
        out_specs=(P(DP, CTX, None), P(DP, CTX, None), P(DP, None, None), P(DP, None), *weights),
        check_vma=False,
    )
```

```python
import jax
import jax.numpy as jnp
from jax import lax
from jax.experimental import pallas as pl
from jax.experimental.pallas import tpu as pltpu
from jax.sharding import Mesh
from jax.sharding import PartitionSpec as P

DP = ("z", "yl")
CTX = ("x", "yh")
PLANE = ("z", "yh", "yl")
SWAP = ((0, 0), (1, 2), (2, 1), (3, 3))

D = 1536
HD = 64
ROT = 32
HEADS = 3
WIDE = 256
V_AT, K_AT, O_AT, QVK = 128, 384, 512, 640
ROWS = 128
SEQ = 1024
QB = 256
CROSS_KEYS = 144
norm_eps = 1e-05
masked_fill = -1e30
bf16 = jnp.bfloat16
f32 = jnp.float32


def permuted(v):
    parts = []
    for z in range(v.shape[-1] // 384):
        for piece in (0, 2, 1, 3):
            at = z * 384 + piece * 96
            parts.append(v[..., at : at + 96])
    return jnp.concatenate(parts, axis=-1)


def dot(a, b):
    return jnp.dot(a, b, preferred_element_type=f32)


def dot_nt(a, b):
    return lax.dot_general(a, b, (((1,), (1,)), ((), ())), preferred_element_type=f32)


def dot_tn(a, b):
    return lax.dot_general(a, b, (((0,), (0,)), ((), ())), preferred_element_type=f32)


def to_partner(v):
    return lax.ppermute(v, "tp", ((0, 1), (1, 0)))


def exchanged(v, axes):
    return lax.all_to_all(v, axes, split_axis=0, concat_axis=0, tiled=True)


def sent_to_all(v, axes, count):
    return exchanged(jnp.broadcast_to(v[None], (count, *v.shape)), axes)


def after(values, *others):
    return lax.optimization_barrier((values, others))[0]


def both(first, *others):
    return lax.optimization_barrier((first, *others))


def along_x(v, step):
    return lax.ppermute(v, "x", [(i, (i + step) % 4) for i in range(4)])


def gather_x(own):
    return [own] + [along_x(own, step) for step in (1, 2, 3)]


def scatter_x(blocks):
    return [blocks[0]] + [along_x(blocks[step], -step) for step in (1, 2, 3)]


def swapped_x(blocks):
    return [blocks[0]] + [along_x(blocks[step], step) for step in (1, 2, 3)]


def summed(blocks):
    return sum(block.astype(f32) for block in blocks[1:]) + blocks[0].astype(f32)


def gather_half(own):
    return jnp.concatenate(gather_x(own), axis=0)


def to_far(v):
    return lax.ppermute(v, "yh", ((0, 1), (1, 0)))


def with_partner(mine):
    return jnp.concatenate([mine, to_partner(mine)], axis=0)


def scatter_half(partial):
    half = 4 * ROWS
    got = to_partner(partial[half:].astype(bf16))
    mine = (partial[:half].astype(f32) + got.astype(f32)).astype(bf16)
    return [mine[k * ROWS : (k + 1) * ROWS] for k in range(4)]


def plane_parts(grad):
    return exchanged(grad.astype(bf16).reshape(16, grad.shape[0] // 16, grad.shape[1]), PLANE)


def total(parts):
    return jnp.sum(parts.astype(f32), axis=0)


def pair_rows(own):
    return jnp.concatenate([own, to_partner(own)], axis=0)


def pair_sum(partial):
    return partial[:ROWS] + to_partner(partial[ROWS:])


def gather_plane(shard):
    return lax.all_gather(shard, PLANE, axis=0, tiled=True)


def scatter_plane(grad):
    return lax.psum_scatter(grad, PLANE, scatter_dimension=0, tiled=True)


def unit_norm(v):
    centered = v - jnp.mean(v, axis=-1, keepdims=True)
    scale = lax.rsqrt(jnp.mean(centered * centered, axis=-1, keepdims=True) + norm_eps)
    return centered * scale, scale


def unit_norm_back(x_hat, scale, grad):
    along = jnp.mean(grad * x_hat, axis=-1, keepdims=True)
    return scale * (grad - jnp.mean(grad, axis=-1, keepdims=True) - x_hat * along)


def lane_masks(rows):
    lane = lax.broadcasted_iota(jnp.int32, (rows, WIDE), 1)
    heads = [(lane // HD == h).astype(f32).astype(bf16) for h in range(HEADS + 1)]
    return lane, heads, (lane == HEADS * HD).astype(f32).astype(bf16)


def turned(v, cosine, sine, first):
    other = jnp.where(first, pltpu.roll(v, WIDE - ROT // 2, 1), pltpu.roll(v, ROT // 2, 1))
    cosine, sine = (jnp.concatenate([table, table], axis=1) for table in (cosine, sine))
    return v * cosine, other * sine


def attn_forward_kernel(sc, qkv, cosine, sine, att, qs, ks, vs, lse, vt):
    lane, heads, extra = lane_masks(QB)
    first = lane % HD < ROT // 2
    value_head = lax.broadcasted_iota(jnp.int32, (WIDE, QB), 0) // HD - 1

    def prepare(block, carry):
        rows = pl.ds(block * QB, QB)
        c, s = cosine[rows, :], sine[rows, :]
        straight, crossed = turned(qkv[rows, 0:WIDE], c, s, first)
        query = ((straight + crossed) * HD ** (-0.5)).astype(bf16)
        qs[rows, :] = jnp.where(lane < HEADS * HD, query.astype(f32), jnp.where(lane == HEADS * HD, 1.0, 0.0)).astype(bf16)
        straight, crossed = turned(qkv[rows, K_AT : K_AT + WIDE], c, s, first)
        row = lax.broadcasted_iota(jnp.int32, (QB, WIDE), 0) + block * QB
        side = jnp.where(row < SEQ // 2, sc[0], 1 - sc[0])
        within = row % (SEQ // 2)
        place = ((sc[2] + 4 - within // ROWS) % 4 * 2 + side) * ROWS + within % ROWS
        fill = jnp.where((lane == HEADS * HD) & (place >= sc[1]), masked_fill, 0.0)
        ks[rows, :] = jnp.where(lane < HEADS * HD, straight + crossed, fill).astype(bf16)
        value = qkv[rows, V_AT : V_AT + WIDE]
        vs[rows, :] = value.astype(bf16)
        vt[:, rows] = value.T.astype(bf16)
        return carry

    for block in range(SEQ // QB):
        prepare(block, 0)

    def attend(block, carry):
        rows = pl.ds(pl.multiple_of(block * QB, QB), QB)
        query = qs[rows, :]
        total = jnp.zeros((WIDE, QB), f32)
        for h in range(HEADS):
            scores = dot_nt(ks[...], query * (heads[h] + extra))
            top = jnp.max(scores, axis=0, keepdims=True)
            weight = jnp.exp(scores - top)
            mass = jnp.sum(weight, axis=0, keepdims=True)
            out = dot(vt[...], weight.astype(bf16))
            total = jnp.where(value_head == h, out / mass, total)
            lse[h : h + 1, rows] = top + jnp.log(mass)
        att[rows, :] = total.T.astype(bf16)
        return carry

    lse[...] = jnp.zeros(lse.shape, f32)
    lax.fori_loop(0, SEQ // QB, attend, 0)


def attn_forward(scalars, qkv, cosine, sine):
    wide = jax.ShapeDtypeStruct((SEQ, WIDE), bf16)
    return pl.pallas_call(
        attn_forward_kernel,
        in_specs=[pl.BlockSpec(memory_space=pltpu.SMEM)] + [pl.BlockSpec(memory_space=pltpu.VMEM)] * 3,
        out_shape=(wide, wide, wide, wide, jax.ShapeDtypeStruct((8, SEQ), f32)),
        scratch_shapes=[pltpu.VMEM((WIDE, SEQ), bf16)],
        cost_estimate=pl.CostEstimate(flops=4 * HEADS * SEQ * SEQ * WIDE, transcendentals=HEADS * SEQ * SEQ, bytes_accessed=8 << 20),
    )(scalars, qkv, cosine, sine)


def attn_backward_kernel(qs, ks, vs, grad, lse, cosine, sine, out, kt, dq, dk, dv):
    lane, heads, extra = lane_masks(QB)
    first = lane % HD < ROT // 2
    wide_head = lax.broadcasted_iota(jnp.int32, (WIDE, QB), 0) // HD
    kept = lane < HEADS * HD
    kt[...] = ks[...].astype(f32).T.astype(bf16)
    dk[...] = jnp.zeros(dk.shape, f32)
    dv[...] = jnp.zeros(dv.shape, f32)

    def step(block, carry):
        rows = pl.ds(pl.multiple_of(block * QB, QB), QB)
        query, given = qs[rows, :], grad[rows, :]
        total = jnp.zeros((WIDE, QB), f32)
        for h in range(HEADS):
            own_query, own_grad = query * heads[h], given * heads[h + 1]
            scores = dot_nt(ks[...], query * (heads[h] + extra))
            weight = jnp.exp(scores - lse[h : h + 1, rows])
            wanted = dot_nt(vs[...], own_grad)
            product = weight * wanted
            inner = jnp.sum(product, axis=0, keepdims=True)
            slope = (product - weight * inner).astype(bf16)
            dv[...] += dot(weight.astype(bf16), own_grad)
            dk[...] += dot(slope, own_query)
            total = jnp.where(wide_head == h, dot(kt[...], slope), total)
        straight, crossed = turned(total.T * HD ** (-0.5), cosine[rows, :], sine[rows, :], first)
        turned_back = straight - crossed
        out[rows, 0:128] = turned_back[:, :128].astype(bf16)
        dq[rows, :] = turned_back[:, 128:]
        return carry

    lax.fori_loop(0, SEQ // QB, step, 0)
    for block in range(SEQ // QB):
        rows = pl.ds(block * QB, QB)
        value = dv[rows, :]
        out[rows, V_AT : V_AT + 128] = jnp.where(lane[:, :128] < HD, dq[rows, :], value[:, :128]).astype(bf16)
        out[rows, V_AT + 128 : V_AT + 256] = value[:, 128:].astype(bf16)
        straight, crossed = turned(dk[rows, :], cosine[rows, :], sine[rows, :], first)
        out[rows, K_AT : K_AT + WIDE] = jnp.where(kept, straight - crossed, 0.0).astype(bf16)


def attn_backward(qs, ks, vs, grad, lse, cosine, sine):
    return pl.pallas_call(
        attn_backward_kernel,
        in_specs=[pl.BlockSpec(memory_space=pltpu.VMEM)] * 7,
        out_shape=jax.ShapeDtypeStruct((SEQ, QVK), bf16),
        scratch_shapes=[pltpu.VMEM((WIDE, SEQ), bf16), pltpu.VMEM((SEQ, 128), f32), pltpu.VMEM((SEQ, WIDE), f32), pltpu.VMEM((SEQ, WIDE), f32)],
        cost_estimate=pl.CostEstimate(flops=10 * HEADS * SEQ * SEQ * WIDE, transcendentals=HEADS * SEQ * SEQ, bytes_accessed=8 << 20),
    )(qs, ks, vs, grad, lse, cosine, sine)


PAIR = 2 * HD
QUARTER = HEADS * HD


def pair_of(sc, kv, group, kind):
    lanes = []
    for head in (2 * group, 2 * group + 1):
        at = kind * QUARTER + head % HEADS * HD
        lanes.append(kv[(sc[2] + 4 - head // HEADS) % 4, :, at : at + HD])
    return jnp.concatenate(lanes, axis=1)


def cross_weights(query, keys, bias):
    scores = dot_nt(keys, query) + bias
    weight = jnp.exp(scores - jnp.max(scores, axis=0, keepdims=True))
    return weight / jnp.sum(weight, axis=0, keepdims=True)


def store_quarters(sc, out, group, value):
    for h in range(2):
        head = 2 * group + h
        at = head % HEADS * HD
        for side in range(2):
            piece = value[side * ROWS : (side + 1) * ROWS, h * HD : (h + 1) * HD]
            out[(head // HEADS + 4 - sc[2]) % 4, 0:ROWS, side * QUARTER + at : side * QUARTER + at + HD] = piece


def cross_forward_kernel(sc, cq, kv, bias, att, quarters):
    lane = lax.broadcasted_iota(jnp.int32, (2 * ROWS, PAIR), 1)
    row = lax.broadcasted_iota(jnp.int32, (PAIR, 2 * ROWS), 0)
    for group in range(cq.shape[1] // PAIR):
        at = pl.ds(group * PAIR, PAIR)
        query, keys = cq[:, at], pair_of(sc, kv, group, 0)
        values = pair_of(sc, kv, group, 1).astype(f32).T.astype(bf16)
        outs = []
        for h in range(2):
            mask = (lane // HD == h).astype(f32).astype(bf16)
            weight = cross_weights(query * mask, keys, bias[...])
            outs.append(dot(values, weight.astype(bf16)))
        value = jnp.where(row < HD, outs[0], outs[1]).T.astype(bf16)
        att[:, at] = value
        store_quarters(sc, quarters, group, value)


def cross_forward(scalars, cq, kv, bias):
    return pl.pallas_call(
        cross_forward_kernel,
        in_specs=[pl.BlockSpec(memory_space=pltpu.SMEM)] + [pl.BlockSpec(memory_space=pltpu.VMEM)] * 3,
        out_shape=(jax.ShapeDtypeStruct(cq.shape, bf16), jax.ShapeDtypeStruct((4, ROWS, 2 * QUARTER), bf16)),
        cost_estimate=pl.CostEstimate(flops=4 * 12 * 256 * 144 * 128, transcendentals=12 * 256 * 144, bytes_accessed=2 << 20),
    )(scalars, cq, kv, bias)


def cross_backward_kernel(sc, cq, kv, bias, grad, dq, quarters):
    lane = lax.broadcasted_iota(jnp.int32, (2 * ROWS, PAIR), 1)
    row = lax.broadcasted_iota(jnp.int32, (PAIR, 2 * ROWS), 0)
    for group in range(cq.shape[1] // PAIR):
        at = pl.ds(group * PAIR, PAIR)
        query, given = cq[:, at], grad[:, at]
        keys, values = pair_of(sc, kv, group, 0), pair_of(sc, kv, group, 1)
        turned_keys = keys.astype(f32).T.astype(bf16)
        outs, grads = [], [0.0, 0.0]
        for h in range(2):
            mask = (lane // HD == h).astype(f32).astype(bf16)
            own_query, own_grad = query * mask, given * mask
            weight = cross_weights(own_query, keys, bias[...])
            product = weight * dot_nt(values, own_grad)
            slope = (product - weight * jnp.sum(product, axis=0, keepdims=True)).astype(bf16)
            outs.append(dot(turned_keys, slope))
            grads[0] += dot(slope, own_query)
            grads[1] += dot(weight.astype(bf16), own_grad)
        value = (jnp.where(row < HD, outs[0], outs[1]).T * HD ** (-0.5)).astype(bf16)
        dq[:, at] = value
        store_quarters(sc, quarters, group, value)
        for h in range(2):
            head = 2 * group + h
            for kind in range(2):
                place = kind * QUARTER + head % HEADS * HD
                piece = grads[kind][:, h * HD : (h + 1) * HD].astype(bf16)
                quarters[(head // HEADS + 4 - sc[2]) % 4, ROWS:, place : place + HD] = piece


def cross_backward(scalars, cq, kv, bias, grad):
    return pl.pallas_call(
        cross_backward_kernel,
        in_specs=[pl.BlockSpec(memory_space=pltpu.SMEM)] + [pl.BlockSpec(memory_space=pltpu.VMEM)] * 4,
        out_shape=(
            jax.ShapeDtypeStruct(cq.shape, bf16),
            jax.ShapeDtypeStruct((4, ROWS + kv.shape[1], 2 * QUARTER), bf16),
        ),
        cost_estimate=pl.CostEstimate(flops=10 * 12 * 256 * 144 * 128, transcendentals=12 * 256 * 144, bytes_accessed=3 << 20),
    )(scalars, cq, kv, bias, grad)


def rotary_lanes(side, x):
    row = jnp.arange(SEQ, dtype=jnp.int32)
    within = row % (SEQ // 2)
    part = jnp.where(row < SEQ // 2, side, 1 - side)
    place = (((x + 4 - within // ROWS) % 4 * 2 + part) * ROWS + within % ROWS).astype(f32)
    lane = jnp.arange(128, dtype=jnp.int32) % HD
    exponent = (lane % (ROT // 2)).astype(f32) * (2.0 / ROT)
    angle = place[:, None] * jnp.power(jnp.float32(10000.0), -exponent)[None, :]
    inside = (lane < ROT)[None, :]
    sign = jnp.where(lane < ROT // 2, -1.0, 1.0)[None, :]
    return jnp.where(inside, jnp.cos(angle), 1.0), jnp.where(inside, jnp.sin(angle) * sign, 0.0)


def products_kernel(count, *refs):
    out, at = refs[-1], 0
    for k in range(count):
        left, right = refs[2 * k], refs[2 * k + 1]
        width = right.shape[1]
        out[:, at : at + width] = dot_tn(left[...], right[...]).astype(bf16)
        at += width


def products(*pairs):
    tile, total_width = 256, sum(right.shape[1] for _, right in pairs)
    flat, specs = [], []
    for left, right in pairs:
        flat += [left, right]
        specs += [pl.BlockSpec((left.shape[0], tile), lambda i: (0, i)), pl.BlockSpec(right.shape, lambda i: (0, 0))]
    work = sum(left.shape[0] * right.shape[1] for left, right in pairs)
    return pl.pallas_call(
        lambda *refs: products_kernel(len(pairs), *refs),
        grid=(D // tile,),
        in_specs=specs,
        out_specs=pl.BlockSpec((tile, total_width), lambda i: (i, 0)),
        out_shape=jax.ShapeDtypeStruct((D, total_width), bf16),
        cost_estimate=pl.CostEstimate(flops=2 * D * work, transcendentals=0, bytes_accessed=10 << 20),
    )(*flat)


def by_rows(blocks, at):
    starts = (at, at + QUARTER)
    return jnp.concatenate([b[:ROWS, k : k + QUARTER] for k in starts for b in blocks], axis=0)


def attn_products_kernel(one, grad, back, att, context, share, two, three, *rest):
    cq, catt, out = rest[:4], rest[4:8], rest[8]
    proj, across = dot_tn(one[...], grad[...]), dot_tn(back[...], att[...])
    out[:, :O_AT] = proj[:, :O_AT].astype(bf16)
    out[:, O_AT:QVK] = (proj[:, O_AT:] + across[:, : QVK - O_AT]).astype(bf16)
    out[:, QVK : O_AT + WIDE] = across[:, QVK - O_AT :].astype(bf16)
    at = O_AT + WIDE
    out[:, at : at + 2 * QUARTER] = dot_tn(context[...], share[...]).astype(bf16)
    at += 2 * QUARTER
    pieces = [dot_tn(two[...], by_rows(cq, 0)).astype(bf16), dot_tn(three[...], by_rows(catt, D)).astype(bf16)]
    out[:, at:] = jnp.concatenate(pieces, axis=1)


def attn_products(one, grad, back, att, context, share, two, three, cq, catt):
    tile, width = 256, O_AT + WIDE + 4 * QUARTER

    def whole(v):
        return pl.BlockSpec(v.shape, lambda i: (0, 0))

    def piece(v):
        return pl.BlockSpec((v.shape[0], tile), lambda i: (0, i))

    specs = [piece(one), whole(grad), piece(back), whole(att), piece(context), whole(share), piece(two), piece(three)]
    return pl.pallas_call(
        attn_products_kernel,
        grid=(D // tile,),
        in_specs=specs + [whole(v) for v in (*cq, *catt)],
        out_specs=pl.BlockSpec((tile, width), lambda i: (i, 0)),
        out_shape=jax.ShapeDtypeStruct((D, width), bf16),
        cost_estimate=pl.CostEstimate(flops=2 * D * SEQ * width, transcendentals=0, bytes_accessed=16 << 20),
    )(one, grad, back, att, context, share, two, three, *cq, *catt)


def held_at(q, x):
    return (x + 4 - q) % 4


def finish_feed_kernel(at, b0, b1, b2, b3, gain, grad_in, grad_down, held):
    rows, width = b0.shape[1], grad_down.shape[1] // 4
    for k, block in enumerate((b0, b1, b2, b3)):
        held[k] = block[...]
    for h in range(2):
        scale = gain[h * rows : (h + 1) * rows, :]
        for q in range(4):
            part = held[held_at(q, at[0]), (at[1] + h) % 2]
            to = pl.ds(q * width, width)
            for kind in range(2):
                grad_in[kind, h * rows : (h + 1) * rows, to] = part[:, kind * width : (kind + 1) * width].astype(f32) * scale
            grad_down[h * rows : (h + 1) * rows, to] = part[:, 2 * width :].astype(f32)


def finish_feed(at, blocks, gain):
    _, rows, columns = blocks[0].shape
    width = columns // 3
    return pl.pallas_call(
        finish_feed_kernel,
        in_specs=[pl.BlockSpec(memory_space=pltpu.SMEM)] + [pl.BlockSpec(memory_space=pltpu.VMEM)] * 5,
        out_shape=(
            jax.ShapeDtypeStruct((2, 2 * rows, 4 * width), f32),
            jax.ShapeDtypeStruct((2 * rows, 4 * width), f32),
        ),
        scratch_shapes=[pltpu.VMEM((4, 2, rows, columns), bf16)],
        cost_estimate=pl.CostEstimate(flops=1 << 22, transcendentals=0, bytes_accessed=11 << 20),
    )(at, *blocks, gain)


def finish_cond_kernel(at, near, far, out):
    width = near.shape[2]
    for q in range(4):
        place = held_at(q, at[0])
        out[at[1], :, q * width : (q + 1) * width] = near[place].astype(f32)
        out[1 - at[1], :, q * width : (q + 1) * width] = far[place].astype(f32)


def finish_cond(at, near, far):
    _, count, width = near.shape
    return pl.pallas_call(
        finish_cond_kernel,
        in_specs=[pl.BlockSpec(memory_space=pltpu.SMEM)] + [pl.BlockSpec(memory_space=pltpu.VMEM)] * 2,
        out_shape=jax.ShapeDtypeStruct((2, count, 4 * width), f32),
        cost_estimate=pl.CostEstimate(flops=1 << 20, transcendentals=0, bytes_accessed=3 << 20),
    )(at, near, far)


def finish_columns_kernel(at, b0, b1, b2, b3, gain, other_gain, proj, out, keyval, query, cross, held):
    rows = b0.shape[1]
    for k, block in enumerate((b0, b1, b2, b3)):
        held[k] = block[...]
    for h in range(2):
        to = pl.ds(h * rows, rows)
        parts = [held[held_at(q, at[0]), (at[1] + h) % 2] for q in range(4)]

        def kind_of(kind):
            row = [part[:, kind * QUARTER : (kind + 1) * QUARTER].astype(f32) for part in parts]
            return jnp.concatenate(row, axis=1)

        for place, kind in enumerate((0, 2, 1)):
            proj[place, to, :] = kind_of(kind) * gain[to, :]
        out[to, :] = kind_of(3)
        keyval[0, to, :] = kind_of(4)
        keyval[1, to, :] = kind_of(5)
        query[to, :] = kind_of(6) * other_gain[to, :]
        cross[to, :] = kind_of(7)


def finish_columns(at, blocks, gain, other_gain):
    _, rows, columns = blocks[0].shape
    width = columns // 2
    plain = jax.ShapeDtypeStruct((2 * rows, width), f32)
    return pl.pallas_call(
        finish_columns_kernel,
        in_specs=[pl.BlockSpec(memory_space=pltpu.SMEM)] + [pl.BlockSpec(memory_space=pltpu.VMEM)] * 6,
        out_shape=(
            jax.ShapeDtypeStruct((3, 2 * rows, width), f32),
            plain,
            jax.ShapeDtypeStruct((2, 2 * rows, width), f32),
            plain,
            plain,
        ),
        scratch_shapes=[pltpu.VMEM((4, 2, rows, columns), bf16)],
        cost_estimate=pl.CostEstimate(flops=1 << 20, transcendentals=0, bytes_accessed=4 << 20),
    )(at, *blocks, gain, other_gain)


def per_device(
    hidden_in,
    context,
    lengths,
    cond_mask,
    out_grad,
    gain_attn,
    self_proj,
    self_out,
    gain_cross,
    cross_query,
    cross_keyval,
    cross_out,
    gain_feed,
    feed_in,
    feed_out,
):
    x, yh, tp = lax.axis_index("x"), lax.axis_index("yh"), lax.axis_index("tp")
    cond_count = context.shape[1]
    own_rows = hidden_in.shape[1]
    half_rows = self_proj.shape[0] // 2
    quarter = self_proj.shape[2] // 4
    hidden_quarter = feed_in.shape[2] // 4
    local_width = self_proj.shape[2]

    def own_half(w):
        return lax.dynamic_slice_in_dim(w, yh * half_rows, half_rows, 0)

    def own_cols(w, count):
        return lax.dynamic_slice_in_dim(w, x * count, count, w.ndim - 1)

    def scaled(w, gain):
        return (w.astype(f32) * own_half(gain).astype(f32)[:, None]).astype(bf16)

    x_own = lax.ppermute(lax.dynamic_index_in_dim(hidden_in, tp, 0, False), ("yh", "tp"), SWAP)
    u_own = lax.ppermute(lax.dynamic_index_in_dim(out_grad, tp, 0, False), ("yh", "tp"), SWAP)
    length = lax.dynamic_index_in_dim(lengths, yh, 0, False)
    own_mask = lax.dynamic_index_in_dim(cond_mask, yh, 0, False)
    tokens = permuted(x_own).astype(f32)
    norm_one, scale_one = unit_norm(tokens)

    qkv_cols = own_cols(own_half(self_proj), quarter)
    qvk_cols = jnp.concatenate([qkv_cols[:, 0], qkv_cols[:, 2], qkv_cols[:, 1]], axis=1)
    out_cols = own_cols(own_half(self_out), quarter)
    keyval_cols = own_cols(own_half(cross_keyval), quarter).reshape(half_rows, 2 * quarter)
    cq_half = own_half(cross_query)
    first_set = gather_plane(
        jnp.concatenate([scaled(qvk_cols, gain_attn), out_cols, keyval_cols, scaled(cq_half, gain_cross), own_half(cross_out)], axis=1)
    )
    sent_one = norm_one.astype(bf16)
    sent_one, feed_in, feed_out, context = both(sent_one, feed_in, feed_out, context)
    feed_cols = own_cols(own_half(feed_in), hidden_quarter).reshape(half_rows, 2 * hidden_quarter)
    down_cols = own_cols(own_half(feed_out), hidden_quarter)
    feed_set = gather_plane(jnp.concatenate([scaled(feed_cols, gain_feed), down_cols], axis=1))
    w_qvk, w_out = first_set[:, :QVK], first_set[:, O_AT : O_AT + WIDE]
    cq_at = O_AT + WIDE + 2 * quarter
    w_kv, w_cq, w_co = first_set[:, O_AT + WIDE : cq_at], first_set[:, cq_at : cq_at + local_width], first_set[:, cq_at + local_width :]
    w_feed, w_down = feed_set[:, : 2 * hidden_quarter], feed_set[:, 2 * hidden_quarter :]

    scalars = jnp.stack([tp.astype(jnp.int32), length, x.astype(jnp.int32)])
    own_context = jnp.pad(lax.dynamic_index_in_dim(context, yh, 0, False), ((0, CROSS_KEYS - cond_count), (0, 0)))
    mine_one, u_own, cosine, sine, own_context = both(
        gather_half(sent_one), u_own, *rotary_lanes(tp, x), permuted(own_context)
    )
    upstream = permuted(u_own)
    full_one, mine_grad = both(with_partner(mine_one), gather_half(upstream))
    qvk, keyval, full_grad = both(dot(full_one, w_qvk), dot(own_context, w_kv).astype(bf16), with_partner(mine_grad))
    attended, qs, ks, vs, lse = attn_forward(scalars, qvk, cosine, sine)
    attended, keyval = both(attended, gather_x(keyval))
    cond_kv = jnp.stack(keyval)
    blocks = both(*scatter_half(dot_nt(attended, w_out)))
    attn_branch = summed(both(*scatter_x(blocks)))
    resid_one = tokens + attn_branch

    seen = jnp.pad(own_mask > 0, (0, CROSS_KEYS - cond_count))
    bias = jnp.broadcast_to(jnp.where(seen, 0.0, masked_fill)[:, None], (CROSS_KEYS, 2 * own_rows)).astype(f32)
    norm_two, scale_two = unit_norm(resid_one)
    sent_two = norm_two.astype(bf16)
    pair_two = pair_rows(sent_two)
    cross_q = (dot(pair_two, w_cq) * HD ** (-0.5)).astype(bf16)
    cross_att, att_quarters = cross_forward(scalars, cross_q, cond_kv, bias)
    cross_branch = pair_sum(dot_nt(cross_att, w_co))
    resid_two = resid_one + cross_branch
    norm_three, scale_three = unit_norm(resid_two)

    sent_three, full_grad, sent_two, att_quarters = both(norm_three.astype(bf16), full_grad, sent_two, att_quarters)
    mine_three, grad_hidden = both(gather_half(sent_three), dot(full_grad, w_down))
    full_three, sent_two, att_quarters = both(with_partner(mine_three), sent_two, att_quarters)
    carried = [jnp.concatenate([sent_two, att_quarters[k]], axis=1) for k in range(4)]
    carried = swapped_x(carried)
    gate_up = dot(full_three, w_feed)
    gate, upward = gate_up[:, :hidden_quarter], gate_up[:, hidden_quarter:]
    sig = jax.nn.sigmoid(gate)
    hidden = (gate * sig * upward).astype(bf16)
    grad_gate = grad_hidden * upward * sig * (1.0 + gate * (1.0 - sig))
    grad_gate_up = jnp.concatenate([grad_gate.astype(bf16), (grad_hidden * gate * sig).astype(bf16)], axis=1)
    partial, carried = both(dot_nt(grad_gate_up, w_feed), carried)
    blocks, carried, grad_gate_up, hidden = both(scatter_half(partial), carried, grad_gate_up, hidden)
    mine_two = jnp.concatenate([block[:, :D] for block in carried], axis=0)
    att_quarter = carried
    grad_three, grad_feed, full_two = both(
        scatter_x(blocks), products((full_three, grad_gate_up), (full_grad, hidden)), with_partner(mine_two)
    )
    sum_feed = scatter_plane(grad_feed)
    grad_resid_two = upstream.astype(f32) + unit_norm_back(norm_three, scale_three, summed(grad_three))

    sent_two = grad_resid_two.astype(bf16)
    mine_two = gather_half(sent_two)
    pair_grad = pair_rows(sent_two)
    grad_cross_att = dot(pair_grad, w_co).astype(bf16)
    grad_cq, quarters = cross_backward(scalars, cross_q, cond_kv, bias, grad_cross_att)
    grad_cq, mine_two = both(grad_cq, mine_two)
    grad_two = pair_sum(dot_nt(grad_cq, w_cq))
    grad_resid_one = grad_resid_two + unit_norm_back(norm_two, scale_two, grad_two)

    sent_back, mine_two, quarters, hidden = both(grad_resid_one.astype(bf16), mine_two, quarters, hidden)
    mine_back, grad_two_all, feed_half = both(
        gather_half(sent_back), with_partner(mine_two), scatter_half(dot_nt(hidden, w_down))
    )
    full_back, quarters, feed_half = both(with_partner(mine_back), quarters, feed_half)
    grad_att, quarters, feed_half = both(dot(full_back, w_out).astype(bf16), quarters, feed_half)
    quarter_parts = swapped_x([quarters[k] for k in range(4)])
    feed_parts = scatter_x(feed_half)
    grad_qvk = attn_backward(qs, ks, vs, grad_att, lse, cosine, sine)
    grad_qvk, quarter_parts, sum_feed = both(grad_qvk, quarter_parts, sum_feed)
    ckv_share = summed([part[ROWS:] for part in quarter_parts]).astype(bf16)
    partial, grad_qvk, ckv_share, sum_feed = both(dot_nt(grad_qvk, w_qvk), grad_qvk, ckv_share, sum_feed)
    grad_attn = attn_products(
        full_one, grad_qvk, full_back, attended, own_context, ckv_share, full_two, grad_two_all, quarter_parts, att_quarter
    )
    blocks, grad_attn, ckv_share, feed_parts, sum_feed_far = both(
        scatter_half(partial), grad_attn, ckv_share, feed_parts, to_far(sum_feed)
    )
    parts_attn = plane_parts(grad_attn)
    feed_all = gather_x(jnp.stack([sum_feed, sum_feed_far]))
    cond_part = dot_nt(ckv_share, w_kv)[:cond_count]
    cond_part = (cond_part + to_partner(cond_part)).astype(bf16)
    feed_branch = summed(feed_parts)
    output = resid_two + feed_branch
    grad_one, cond_part, sent_out = both(scatter_x(blocks), cond_part, permuted(output.astype(bf16)))
    in_grad = grad_resid_one + unit_norm_back(norm_one, scale_one, summed(grad_one))

    def columns_of(back):
        return lax.dynamic_slice_in_dim(cond_part, (x + 4 - back) % 4 * (D // 4), D // 4, 1)

    cond_parts = scatter_x([columns_of(back) for back in range(4)])
    cond_near = jnp.stack(gather_x(permuted(summed(cond_parts).astype(bf16))))
    at = jnp.stack([x, yh]).astype(jnp.int32)

    def column(gain):
        return gain.astype(f32)[:, None]

    grad_feed_in, grad_feed_out = finish_feed(at, feed_all, column(gain_feed))
    grad_feed_in = grad_feed_in.transpose(1, 0, 2)

    def row_sums(w, grad):
        sums = jnp.sum(w.astype(f32) * grad.astype(f32), axis=1)
        return jnp.pad(sums, (0, 128 - half_rows))

    row = jnp.arange(own_rows, dtype=jnp.int32)
    valid = ((2 * x + tp) * own_rows + row < length)[:, None]
    squares = [jnp.sum(jnp.where(valid, v * v, 0.0)) for v in (tokens, attn_branch, cross_branch, feed_branch, output)]
    small = jnp.concatenate([row_sums(feed_cols, sum_feed[:, : 2 * hidden_quarter]), jnp.pad(jnp.stack(squares), (0, 123))])

    moved_in = lax.ppermute(permuted(in_grad.astype(bf16)), ("yh", "tp"), SWAP)
    moved_out = lax.ppermute(sent_out, ("yh", "tp"), SWAP)
    parts_attn, moved_in, moved_out, small, cond_near, grad_feed_in, grad_feed_out = both(
        parts_attn, moved_in, moved_out, small, cond_near, grad_feed_in, grad_feed_out
    )
    sum_attn = total(parts_attn)
    attn_own, cond_near = both(sum_attn.astype(bf16), cond_near)
    attn_far = to_far(attn_own)
    attn_all = gather_x(jnp.stack([attn_own, attn_far]))
    more = [row_sums(qvk_cols, sum_attn[:, : 3 * quarter])]
    more += [row_sums(own_cols(cq_half, quarter), sum_attn[:, 6 * quarter : 7 * quarter])]
    small = jnp.concatenate([*more, small]).reshape(4, 128)
    small_blocks = gather_x(small + to_partner(small))
    in_grad = lax.all_gather(moved_in, "tp", axis=0, tiled=False).astype(f32)
    layer_out = lax.all_gather(moved_out, "tp", axis=0, tiled=False)
    cond_grad = finish_cond(at, cond_near, to_far(cond_near))
    attn_all, small_blocks, cond_grad, in_grad, layer_out = both(attn_all, small_blocks, cond_grad, in_grad, layer_out)
    proj, out, keyval, query, cross = finish_columns(at, attn_all, column(gain_attn), column(gain_cross))
    small = jnp.stack(small_blocks)
    small = sum(lax.dynamic_index_in_dim(small, (x + 4 - q) % 4, 0, False) for q in range(4))
    other = lax.ppermute(small, "yh", ((0, 1), (1, 0)))
    small = jnp.where(yh == 0, jnp.stack([small, other]), jnp.stack([other, small]))
    layer_stats = jnp.sqrt(small[:, 3, :5] / (lengths.astype(f32)[:, None] * D))
    gains = [small[:, k, :half_rows].reshape(2 * half_rows) for k in range(3)]

    return (
        layer_out,
        in_grad,
        cond_grad,
        layer_stats,
        gains[0],
        proj.transpose(1, 0, 2),
        out,
        gains[1],
        query,
        keyval.transpose(1, 0, 2),
        cross,
        gains[2],
        grad_feed_in,
        grad_feed_out,
    )


def solution(mesh):
    fine = Mesh(mesh.devices.reshape(4, 2, 4, 2, 2), ("z", "yl", "x", "yh", "tp"))
    weights = (
        P(DP),
        P(DP, None, "tp"),
        P(DP, "tp"),
        P(DP),
        P(DP, "tp"),
        P(DP, None, "tp"),
        P(DP, "tp"),
        P(DP),
        P(DP, None, "tp"),
        P(DP, "tp"),
    )
    return jax.shard_map(
        per_device,
        mesh=fine,
        in_specs=(P(DP, CTX, None), P(DP, None, None), P(DP), P(DP, None), P(DP, CTX, None), *weights),
        out_specs=(P(DP, CTX, None), P(DP, CTX, None), P(DP, None, None), P(DP, None), *weights),
        check_vma=False,
    )
```

```python
import jax
import jax.numpy as jnp
from jax import lax
from jax.experimental import pallas as pl
from jax.experimental.pallas import tpu as pltpu
from jax.sharding import Mesh
from jax.sharding import PartitionSpec as P

DP = ("z", "yl")
CTX = ("x", "yh")
PLANE = ("z", "yh", "yl")
SWAP = ((0, 0), (1, 2), (2, 1), (3, 3))

D = 1536
HD = 64
ROT = 32
HEADS = 3
WIDE = 256
V_AT, K_AT, O_AT, QVK = 128, 384, 512, 640
ROWS = 128
SEQ = 1024
QB = 256
CROSS_KEYS = 144
norm_eps = 1e-05
masked_fill = -1e30
bf16 = jnp.bfloat16
f32 = jnp.float32


def permuted(v):
    parts = []
    for z in range(v.shape[-1] // 384):
        for piece in (0, 2, 1, 3):
            at = z * 384 + piece * 96
            parts.append(v[..., at : at + 96])
    return jnp.concatenate(parts, axis=-1)


def dot(a, b):
    return jnp.dot(a, b, preferred_element_type=f32)


def dot_nt(a, b):
    return lax.dot_general(a, b, (((1,), (1,)), ((), ())), preferred_element_type=f32)


def dot_tn(a, b):
    return lax.dot_general(a, b, (((0,), (0,)), ((), ())), preferred_element_type=f32)


def to_partner(v):
    return lax.ppermute(v, "tp", ((0, 1), (1, 0)))


def exchanged(v, axes):
    return lax.all_to_all(v, axes, split_axis=0, concat_axis=0, tiled=True)


def sent_to_all(v, axes, count):
    return exchanged(jnp.broadcast_to(v[None], (count, *v.shape)), axes)


def after(values, *others):
    return lax.optimization_barrier((values, others))[0]


def both(first, *others):
    return lax.optimization_barrier((first, *others))


def along_x(v, step):
    return lax.ppermute(v, "x", [(i, (i + step) % 4) for i in range(4)])


def gather_x(own):
    return [own] + [along_x(own, step) for step in (1, 2, 3)]


def scatter_x(blocks):
    return [blocks[0]] + [along_x(blocks[step], -step) for step in (1, 2, 3)]


def swapped_x(blocks):
    return [blocks[0]] + [along_x(blocks[step], step) for step in (1, 2, 3)]


def summed(blocks):
    return sum(block.astype(f32) for block in blocks[1:]) + blocks[0].astype(f32)


def gather_half(own):
    return jnp.concatenate(gather_x(own), axis=0)


def to_far(v):
    return lax.ppermute(v, "yh", ((0, 1), (1, 0)))


def with_partner(mine):
    return jnp.concatenate([mine, to_partner(mine)], axis=0)


def halves_sum(near, far):
    mine = (near.astype(f32) + to_partner(far).astype(f32)).astype(bf16)
    return [mine[k * ROWS : (k + 1) * ROWS] for k in range(4)]


def scatter_half(partial):
    half = 4 * ROWS
    return halves_sum(partial[:half], partial[half:].astype(bf16))


def plane_parts(grad):
    return exchanged(grad.astype(bf16).reshape(16, grad.shape[0] // 16, grad.shape[1]), PLANE)


def total(parts):
    return jnp.sum(parts.astype(f32), axis=0)


def pair_rows(own):
    return jnp.concatenate([own, to_partner(own)], axis=0)


def pair_sum(partial):
    return partial[:ROWS] + to_partner(partial[ROWS:])


def gather_plane(shard):
    return lax.all_gather(shard, PLANE, axis=0, tiled=True)


def scatter_plane(grad):
    return lax.psum_scatter(grad, PLANE, scatter_dimension=0, tiled=True)


def unit_norm(v):
    centered = v - jnp.mean(v, axis=-1, keepdims=True)
    scale = lax.rsqrt(jnp.mean(centered * centered, axis=-1, keepdims=True) + norm_eps)
    return centered * scale, scale


def unit_norm_back(x_hat, scale, grad):
    along = jnp.mean(grad * x_hat, axis=-1, keepdims=True)
    return scale * (grad - jnp.mean(grad, axis=-1, keepdims=True) - x_hat * along)


def lane_masks(rows):
    lane = lax.broadcasted_iota(jnp.int32, (rows, WIDE), 1)
    heads = [(lane // HD == h).astype(f32).astype(bf16) for h in range(HEADS + 1)]
    return lane, heads, (lane == HEADS * HD).astype(f32).astype(bf16)


def turned(v, cosine, sine, first):
    other = jnp.where(first, pltpu.roll(v, WIDE - ROT // 2, 1), pltpu.roll(v, ROT // 2, 1))
    cosine, sine = (jnp.concatenate([table, table], axis=1) for table in (cosine, sine))
    return v * cosine, other * sine


def attn_forward_kernel(sc, qkv, cosine, sine, att, qs, ks, vs, lse, vt):
    lane, heads, extra = lane_masks(QB)
    first = lane % HD < ROT // 2
    value_head = lax.broadcasted_iota(jnp.int32, (WIDE, QB), 0) // HD - 1

    def prepare(block, carry):
        rows = pl.ds(block * QB, QB)
        c, s = cosine[rows, :], sine[rows, :]
        straight, crossed = turned(qkv[rows, 0:WIDE], c, s, first)
        query = ((straight + crossed) * HD ** (-0.5)).astype(bf16)
        qs[rows, :] = jnp.where(lane < HEADS * HD, query.astype(f32), jnp.where(lane == HEADS * HD, 1.0, 0.0)).astype(bf16)
        straight, crossed = turned(qkv[rows, K_AT : K_AT + WIDE], c, s, first)
        row = lax.broadcasted_iota(jnp.int32, (QB, WIDE), 0) + block * QB
        side = jnp.where(row < SEQ // 2, sc[0], 1 - sc[0])
        within = row % (SEQ // 2)
        place = ((sc[2] + 4 - within // ROWS) % 4 * 2 + side) * ROWS + within % ROWS
        fill = jnp.where((lane == HEADS * HD) & (place >= sc[1]), masked_fill, 0.0)
        ks[rows, :] = jnp.where(lane < HEADS * HD, straight + crossed, fill).astype(bf16)
        value = qkv[rows, V_AT : V_AT + WIDE]
        vs[rows, :] = value.astype(bf16)
        vt[:, rows] = value.T.astype(bf16)
        return carry

    for block in range(SEQ // QB):
        prepare(block, 0)

    def attend(block, carry):
        rows = pl.ds(pl.multiple_of(block * QB, QB), QB)
        query = qs[rows, :]
        total = jnp.zeros((WIDE, QB), f32)
        for h in range(HEADS):
            scores = dot_nt(ks[...], query * (heads[h] + extra))
            top = jnp.max(scores, axis=0, keepdims=True)
            weight = jnp.exp(scores - top)
            mass = jnp.sum(weight, axis=0, keepdims=True)
            out = dot(vt[...], weight.astype(bf16))
            total = jnp.where(value_head == h, out / mass, total)
            lse[h : h + 1, rows] = top + jnp.log(mass)
        att[rows, :] = total.T.astype(bf16)
        return carry

    lse[...] = jnp.zeros(lse.shape, f32)
    lax.fori_loop(0, SEQ // QB, attend, 0)


def attn_forward(scalars, qkv, cosine, sine):
    wide = jax.ShapeDtypeStruct((SEQ, WIDE), bf16)
    return pl.pallas_call(
        attn_forward_kernel,
        in_specs=[pl.BlockSpec(memory_space=pltpu.SMEM)] + [pl.BlockSpec(memory_space=pltpu.VMEM)] * 3,
        out_shape=(wide, wide, wide, wide, jax.ShapeDtypeStruct((8, SEQ), f32)),
        scratch_shapes=[pltpu.VMEM((WIDE, SEQ), bf16)],
        cost_estimate=pl.CostEstimate(flops=4 * HEADS * SEQ * SEQ * WIDE, transcendentals=HEADS * SEQ * SEQ, bytes_accessed=8 << 20),
    )(scalars, qkv, cosine, sine)


def attn_backward_kernel(qs, ks, vs, grad, lse, cosine, sine, out, kt, dq, dk, dv):
    lane, heads, extra = lane_masks(QB)
    first = lane % HD < ROT // 2
    wide_head = lax.broadcasted_iota(jnp.int32, (WIDE, QB), 0) // HD
    kept = lane < HEADS * HD
    kt[...] = ks[...].astype(f32).T.astype(bf16)
    dk[...] = jnp.zeros(dk.shape, f32)
    dv[...] = jnp.zeros(dv.shape, f32)

    def step(block, carry):
        rows = pl.ds(pl.multiple_of(block * QB, QB), QB)
        query, given = qs[rows, :], grad[rows, :]
        total = jnp.zeros((WIDE, QB), f32)
        for h in range(HEADS):
            own_query, own_grad = query * heads[h], given * heads[h + 1]
            scores = dot_nt(ks[...], query * (heads[h] + extra))
            weight = jnp.exp(scores - lse[h : h + 1, rows])
            wanted = dot_nt(vs[...], own_grad)
            product = weight * wanted
            inner = jnp.sum(product, axis=0, keepdims=True)
            slope = (product - weight * inner).astype(bf16)
            dv[...] += dot(weight.astype(bf16), own_grad)
            dk[...] += dot(slope, own_query)
            total = jnp.where(wide_head == h, dot(kt[...], slope), total)
        straight, crossed = turned(total.T * HD ** (-0.5), cosine[rows, :], sine[rows, :], first)
        turned_back = straight - crossed
        out[rows, 0:128] = turned_back[:, :128].astype(bf16)
        dq[rows, :] = turned_back[:, 128:]
        return carry

    lax.fori_loop(0, SEQ // QB, step, 0)
    for block in range(SEQ // QB):
        rows = pl.ds(block * QB, QB)
        value = dv[rows, :]
        out[rows, V_AT : V_AT + 128] = jnp.where(lane[:, :128] < HD, dq[rows, :], value[:, :128]).astype(bf16)
        out[rows, V_AT + 128 : V_AT + 256] = value[:, 128:].astype(bf16)
        straight, crossed = turned(dk[rows, :], cosine[rows, :], sine[rows, :], first)
        out[rows, K_AT : K_AT + WIDE] = jnp.where(kept, straight - crossed, 0.0).astype(bf16)


def attn_backward(qs, ks, vs, grad, lse, cosine, sine):
    return pl.pallas_call(
        attn_backward_kernel,
        in_specs=[pl.BlockSpec(memory_space=pltpu.VMEM)] * 7,
        out_shape=jax.ShapeDtypeStruct((SEQ, QVK), bf16),
        scratch_shapes=[pltpu.VMEM((WIDE, SEQ), bf16), pltpu.VMEM((SEQ, 128), f32), pltpu.VMEM((SEQ, WIDE), f32), pltpu.VMEM((SEQ, WIDE), f32)],
        cost_estimate=pl.CostEstimate(flops=10 * HEADS * SEQ * SEQ * WIDE, transcendentals=HEADS * SEQ * SEQ, bytes_accessed=8 << 20),
    )(qs, ks, vs, grad, lse, cosine, sine)


PAIR = 2 * HD
QUARTER = HEADS * HD


def pair_of(sc, kv, group, kind):
    lanes = []
    for head in (2 * group, 2 * group + 1):
        at = kind * QUARTER + head % HEADS * HD
        lanes.append(kv[(sc[2] + 4 - head // HEADS) % 4, :, at : at + HD])
    return jnp.concatenate(lanes, axis=1)


def cross_weights(query, keys, bias):
    scores = dot_nt(keys, query) + bias
    weight = jnp.exp(scores - jnp.max(scores, axis=0, keepdims=True))
    return weight / jnp.sum(weight, axis=0, keepdims=True)


def store_quarters(sc, out, group, value):
    for h in range(2):
        head = 2 * group + h
        at = head % HEADS * HD
        for side in range(2):
            piece = value[side * ROWS : (side + 1) * ROWS, h * HD : (h + 1) * HD]
            out[(head // HEADS + 4 - sc[2]) % 4, 0:ROWS, side * QUARTER + at : side * QUARTER + at + HD] = piece


def cross_forward_kernel(sc, cq, kv, bias, att, quarters):
    lane = lax.broadcasted_iota(jnp.int32, (2 * ROWS, PAIR), 1)
    row = lax.broadcasted_iota(jnp.int32, (PAIR, 2 * ROWS), 0)
    for group in range(cq.shape[1] // PAIR):
        at = pl.ds(group * PAIR, PAIR)
        query, keys = cq[:, at], pair_of(sc, kv, group, 0)
        values = pair_of(sc, kv, group, 1).astype(f32).T.astype(bf16)
        outs = []
        for h in range(2):
            mask = (lane // HD == h).astype(f32).astype(bf16)
            weight = cross_weights(query * mask, keys, bias[...])
            outs.append(dot(values, weight.astype(bf16)))
        value = jnp.where(row < HD, outs[0], outs[1]).T.astype(bf16)
        att[:, at] = value
        store_quarters(sc, quarters, group, value)


def cross_forward(scalars, cq, kv, bias):
    return pl.pallas_call(
        cross_forward_kernel,
        in_specs=[pl.BlockSpec(memory_space=pltpu.SMEM)] + [pl.BlockSpec(memory_space=pltpu.VMEM)] * 3,
        out_shape=(jax.ShapeDtypeStruct(cq.shape, bf16), jax.ShapeDtypeStruct((4, ROWS, 2 * QUARTER), bf16)),
        cost_estimate=pl.CostEstimate(flops=4 * 12 * 256 * 144 * 128, transcendentals=12 * 256 * 144, bytes_accessed=2 << 20),
    )(scalars, cq, kv, bias)


def cross_backward_kernel(sc, cq, kv, bias, grad, dq, quarters):
    lane = lax.broadcasted_iota(jnp.int32, (2 * ROWS, PAIR), 1)
    row = lax.broadcasted_iota(jnp.int32, (PAIR, 2 * ROWS), 0)
    for group in range(cq.shape[1] // PAIR):
        at = pl.ds(group * PAIR, PAIR)
        query, given = cq[:, at], grad[:, at]
        keys, values = pair_of(sc, kv, group, 0), pair_of(sc, kv, group, 1)
        turned_keys = keys.astype(f32).T.astype(bf16)
        outs, grads = [], [0.0, 0.0]
        for h in range(2):
            mask = (lane // HD == h).astype(f32).astype(bf16)
            own_query, own_grad = query * mask, given * mask
            weight = cross_weights(own_query, keys, bias[...])
            product = weight * dot_nt(values, own_grad)
            slope = (product - weight * jnp.sum(product, axis=0, keepdims=True)).astype(bf16)
            outs.append(dot(turned_keys, slope))
            grads[0] += dot(slope, own_query)
            grads[1] += dot(weight.astype(bf16), own_grad)
        value = (jnp.where(row < HD, outs[0], outs[1]).T * HD ** (-0.5)).astype(bf16)
        dq[:, at] = value
        store_quarters(sc, quarters, group, value)
        for h in range(2):
            head = 2 * group + h
            for kind in range(2):
                place = kind * QUARTER + head % HEADS * HD
                piece = grads[kind][:, h * HD : (h + 1) * HD].astype(bf16)
                quarters[(head // HEADS + 4 - sc[2]) % 4, ROWS:, place : place + HD] = piece


def cross_backward(scalars, cq, kv, bias, grad):
    return pl.pallas_call(
        cross_backward_kernel,
        in_specs=[pl.BlockSpec(memory_space=pltpu.SMEM)] + [pl.BlockSpec(memory_space=pltpu.VMEM)] * 4,
        out_shape=(
            jax.ShapeDtypeStruct(cq.shape, bf16),
            jax.ShapeDtypeStruct((4, ROWS + kv.shape[1], 2 * QUARTER), bf16),
        ),
        cost_estimate=pl.CostEstimate(flops=10 * 12 * 256 * 144 * 128, transcendentals=12 * 256 * 144, bytes_accessed=3 << 20),
    )(scalars, cq, kv, bias, grad)


def rotary_lanes(side, x):
    row = jnp.arange(SEQ, dtype=jnp.int32)
    within = row % (SEQ // 2)
    part = jnp.where(row < SEQ // 2, side, 1 - side)
    place = (((x + 4 - within // ROWS) % 4 * 2 + part) * ROWS + within % ROWS).astype(f32)
    lane = jnp.arange(128, dtype=jnp.int32) % HD
    exponent = (lane % (ROT // 2)).astype(f32) * (2.0 / ROT)
    angle = place[:, None] * jnp.power(jnp.float32(10000.0), -exponent)[None, :]
    inside = (lane < ROT)[None, :]
    sign = jnp.where(lane < ROT // 2, -1.0, 1.0)[None, :]
    return jnp.where(inside, jnp.cos(angle), 1.0), jnp.where(inside, jnp.sin(angle) * sign, 0.0)


def products_kernel(count, *refs):
    out, at = refs[-1], 0
    for k in range(count):
        left, right = refs[2 * k], refs[2 * k + 1]
        width = right.shape[1]
        out[:, at : at + width] = dot_tn(left[...], right[...]).astype(bf16)
        at += width


def products(*pairs):
    tile, total_width = 256, sum(right.shape[1] for _, right in pairs)
    flat, specs = [], []
    for left, right in pairs:
        flat += [left, right]
        specs += [pl.BlockSpec((left.shape[0], tile), lambda i: (0, i)), pl.BlockSpec(right.shape, lambda i: (0, 0))]
    work = sum(left.shape[0] * right.shape[1] for left, right in pairs)
    return pl.pallas_call(
        lambda *refs: products_kernel(len(pairs), *refs),
        grid=(D // tile,),
        in_specs=specs,
        out_specs=pl.BlockSpec((tile, total_width), lambda i: (i, 0)),
        out_shape=jax.ShapeDtypeStruct((D, total_width), bf16),
        cost_estimate=pl.CostEstimate(flops=2 * D * work, transcendentals=0, bytes_accessed=10 << 20),
    )(*flat)


def by_rows(blocks, at):
    starts = (at, at + QUARTER)
    return jnp.concatenate([b[:ROWS, k : k + QUARTER] for k in starts for b in blocks], axis=0)


def attn_products_kernel(one, grad, back, att, context, share, two, three, *rest):
    cq, catt, out = rest[:4], rest[4:8], rest[8]
    proj, across = dot_tn(one[...], grad[...]), dot_tn(back[...], att[...])
    out[:, :O_AT] = proj[:, :O_AT].astype(bf16)
    out[:, O_AT:QVK] = (proj[:, O_AT:] + across[:, : QVK - O_AT]).astype(bf16)
    out[:, QVK : O_AT + WIDE] = across[:, QVK - O_AT :].astype(bf16)
    at = O_AT + WIDE
    out[:, at : at + 2 * QUARTER] = dot_tn(context[...], share[...]).astype(bf16)
    at += 2 * QUARTER
    pieces = [dot_tn(two[...], by_rows(cq, 0)).astype(bf16), dot_tn(three[...], by_rows(catt, D)).astype(bf16)]
    out[:, at:] = jnp.concatenate(pieces, axis=1)


def attn_products(one, grad, back, att, context, share, two, three, cq, catt):
    tile, width = 256, O_AT + WIDE + 4 * QUARTER

    def whole(v):
        return pl.BlockSpec(v.shape, lambda i: (0, 0))

    def piece(v):
        return pl.BlockSpec((v.shape[0], tile), lambda i: (0, i))

    specs = [piece(one), whole(grad), piece(back), whole(att), piece(context), whole(share), piece(two), piece(three)]
    return pl.pallas_call(
        attn_products_kernel,
        grid=(D // tile,),
        in_specs=specs + [whole(v) for v in (*cq, *catt)],
        out_specs=pl.BlockSpec((tile, width), lambda i: (i, 0)),
        out_shape=jax.ShapeDtypeStruct((D, width), bf16),
        cost_estimate=pl.CostEstimate(flops=2 * D * SEQ * width, transcendentals=0, bytes_accessed=16 << 20),
    )(one, grad, back, att, context, share, two, three, *cq, *catt)


def held_at(q, x):
    return (x + 4 - q) % 4


def finish_feed_kernel(at, *refs):
    blocks, (gain, grad_in, grad_down, held) = refs[:8], refs[8:]
    rows, width = blocks[0].shape[0], grad_down.shape[1] // 4
    for k, block in enumerate(blocks):
        held[k % 4, k // 4] = block[...]
    for h in range(2):
        scale = gain[h * rows : (h + 1) * rows, :]
        for q in range(4):
            part = held[held_at(q, at[0]), (at[1] + h) % 2]
            to = pl.ds(q * width, width)
            for kind in range(2):
                grad_in[h * rows : (h + 1) * rows, kind, to] = part[:, kind * width : (kind + 1) * width].astype(f32) * scale
            grad_down[h * rows : (h + 1) * rows, to] = part[:, 2 * width :].astype(f32)


def finish_feed(at, blocks, gain):
    rows, columns = blocks[0].shape
    width = columns // 3
    return pl.pallas_call(
        finish_feed_kernel,
        in_specs=[pl.BlockSpec(memory_space=pltpu.SMEM)] + [pl.BlockSpec(memory_space=pltpu.VMEM)] * 9,
        out_shape=(
            jax.ShapeDtypeStruct((2 * rows, 2, 4 * width), f32),
            jax.ShapeDtypeStruct((2 * rows, 4 * width), f32),
        ),
        scratch_shapes=[pltpu.VMEM((4, 2, rows, columns), bf16)],
        cost_estimate=pl.CostEstimate(flops=1 << 22, transcendentals=0, bytes_accessed=11 << 20),
    )(at, *blocks, gain)


def finish_cond_kernel(at, near, far, out):
    width = near.shape[2]
    for q in range(4):
        place = held_at(q, at[0])
        near_block, far_block = near[place].astype(f32), far[place].astype(f32)
        for h in range(2):
            out[:, h, q * width : (q + 1) * width] = jnp.where(at[1] == h, near_block, far_block)


def finish_cond(at, near, far):
    _, count, width = near.shape
    return pl.pallas_call(
        finish_cond_kernel,
        in_specs=[pl.BlockSpec(memory_space=pltpu.SMEM)] + [pl.BlockSpec(memory_space=pltpu.VMEM)] * 2,
        out_shape=jax.ShapeDtypeStruct((count, 2, 4 * width), f32),
        cost_estimate=pl.CostEstimate(flops=1 << 20, transcendentals=0, bytes_accessed=3 << 20),
    )(at, near, far)


def finish_columns_kernel(at, *refs):
    blocks, (gain, other_gain, proj, out, keyval, query, cross, held) = refs[:8], refs[8:]
    rows = blocks[0].shape[0]
    for k, block in enumerate(blocks):
        held[k % 4, k // 4] = block[...]
    for h in range(2):
        to = pl.ds(h * rows, rows)
        parts = [held[held_at(q, at[0]), (at[1] + h) % 2] for q in range(4)]

        def kind_of(kind):
            row = [part[:, kind * QUARTER : (kind + 1) * QUARTER].astype(f32) for part in parts]
            return jnp.concatenate(row, axis=1)

        for place, kind in enumerate((0, 2, 1)):
            proj[place, to, :] = kind_of(kind) * gain[to, :]
        out[to, :] = kind_of(3)
        keyval[to, 0, :] = kind_of(4)
        keyval[to, 1, :] = kind_of(5)
        query[to, :] = kind_of(6) * other_gain[to, :]
        cross[to, :] = kind_of(7)


def finish_columns(at, blocks, gain, other_gain):
    rows, columns = blocks[0].shape
    width = columns // 2
    plain = jax.ShapeDtypeStruct((2 * rows, width), f32)
    return pl.pallas_call(
        finish_columns_kernel,
        in_specs=[pl.BlockSpec(memory_space=pltpu.SMEM)] + [pl.BlockSpec(memory_space=pltpu.VMEM)] * 10,
        out_shape=(
            jax.ShapeDtypeStruct((3, 2 * rows, width), f32),
            plain,
            jax.ShapeDtypeStruct((2 * rows, 2, width), f32),
            plain,
            plain,
        ),
        scratch_shapes=[pltpu.VMEM((4, 2, rows, columns), bf16)],
        cost_estimate=pl.CostEstimate(flops=1 << 20, transcendentals=0, bytes_accessed=4 << 20),
    )(at, *blocks, gain, other_gain)


def per_device(
    hidden_in,
    context,
    lengths,
    cond_mask,
    out_grad,
    gain_attn,
    self_proj,
    self_out,
    gain_cross,
    cross_query,
    cross_keyval,
    cross_out,
    gain_feed,
    feed_in,
    feed_out,
):
    x, yh, tp = lax.axis_index("x"), lax.axis_index("yh"), lax.axis_index("tp")
    cond_count = context.shape[1]
    own_rows = hidden_in.shape[1]
    half_rows = self_proj.shape[0] // 2
    quarter = self_proj.shape[2] // 4
    hidden_quarter = feed_in.shape[2] // 4
    local_width = self_proj.shape[2]

    def own_half(w):
        return lax.dynamic_slice_in_dim(w, yh * half_rows, half_rows, 0)

    def own_cols(w, count):
        return lax.dynamic_slice_in_dim(w, x * count, count, w.ndim - 1)

    def scaled(w, gain):
        return (w.astype(f32) * own_half(gain).astype(f32)[:, None]).astype(bf16)

    x_own = lax.ppermute(lax.dynamic_index_in_dim(hidden_in, tp, 0, False), ("yh", "tp"), SWAP)
    u_own = lax.ppermute(lax.dynamic_index_in_dim(out_grad, tp, 0, False), ("yh", "tp"), SWAP)
    length = lax.dynamic_index_in_dim(lengths, yh, 0, False)
    own_mask = lax.dynamic_index_in_dim(cond_mask, yh, 0, False)
    tokens = permuted(x_own).astype(f32)
    norm_one, scale_one = unit_norm(tokens)

    qkv_cols = own_cols(own_half(self_proj), quarter)
    qvk_cols = jnp.concatenate([qkv_cols[:, 0], qkv_cols[:, 2], qkv_cols[:, 1]], axis=1)
    out_cols = own_cols(own_half(self_out), quarter)
    keyval_cols = own_cols(own_half(cross_keyval), quarter).reshape(half_rows, 2 * quarter)
    cq_half = own_half(cross_query)
    first_set = gather_plane(
        jnp.concatenate([scaled(qvk_cols, gain_attn), out_cols, keyval_cols, scaled(cq_half, gain_cross), own_half(cross_out)], axis=1)
    )
    sent_one = norm_one.astype(bf16)
    sent_one, feed_in, feed_out, context = both(sent_one, feed_in, feed_out, context)
    feed_cols = own_cols(own_half(feed_in), hidden_quarter).reshape(half_rows, 2 * hidden_quarter)
    down_cols = own_cols(own_half(feed_out), hidden_quarter)
    feed_set = gather_plane(jnp.concatenate([scaled(feed_cols, gain_feed), down_cols], axis=1))
    w_qvk, w_out = first_set[:, :QVK], first_set[:, O_AT : O_AT + WIDE]
    cq_at = O_AT + WIDE + 2 * quarter
    w_kv, w_cq, w_co = first_set[:, O_AT + WIDE : cq_at], first_set[:, cq_at : cq_at + local_width], first_set[:, cq_at + local_width :]
    w_feed, w_down = feed_set[:, : 2 * hidden_quarter], feed_set[:, 2 * hidden_quarter :]

    scalars = jnp.stack([tp.astype(jnp.int32), length, x.astype(jnp.int32)])
    own_context = jnp.pad(lax.dynamic_index_in_dim(context, yh, 0, False), ((0, CROSS_KEYS - cond_count), (0, 0)))
    mine_one, u_own, cosine, sine, own_context = both(
        gather_half(sent_one), u_own, *rotary_lanes(tp, x), permuted(own_context)
    )
    upstream = permuted(u_own)
    full_one, mine_grad = both(with_partner(mine_one), gather_half(upstream))
    qvk, keyval, full_grad = both(dot(full_one, w_qvk), dot(own_context, w_kv).astype(bf16), with_partner(mine_grad))
    attended, qs, ks, vs, lse = attn_forward(scalars, qvk, cosine, sine)
    attended, keyval = both(attended, gather_x(keyval))
    cond_kv = jnp.stack(keyval)
    blocks = both(*scatter_half(dot_nt(attended, w_out)))
    attn_branch = summed(both(*scatter_x(blocks)))
    resid_one = tokens + attn_branch

    seen = jnp.pad(own_mask > 0, (0, CROSS_KEYS - cond_count))
    bias = jnp.broadcast_to(jnp.where(seen, 0.0, masked_fill)[:, None], (CROSS_KEYS, 2 * own_rows)).astype(f32)
    norm_two, scale_two = unit_norm(resid_one)
    sent_two = norm_two.astype(bf16)
    pair_two = pair_rows(sent_two)
    cross_q = (dot(pair_two, w_cq) * HD ** (-0.5)).astype(bf16)
    cross_att, att_quarters = cross_forward(scalars, cross_q, cond_kv, bias)
    cross_branch = pair_sum(dot_nt(cross_att, w_co))
    resid_two = resid_one + cross_branch
    norm_three, scale_three = unit_norm(resid_two)

    sent_three, full_grad, sent_two, att_quarters = both(norm_three.astype(bf16), full_grad, sent_two, att_quarters)
    mine_three, grad_hidden = both(gather_half(sent_three), dot(full_grad, w_down))
    full_three, sent_two, att_quarters = both(with_partner(mine_three), sent_two, att_quarters)
    carried = [jnp.concatenate([sent_two, att_quarters[k]], axis=1) for k in range(4)]
    carried = swapped_x(carried)
    gate_up = dot(full_three, w_feed)
    gate, upward = gate_up[:, :hidden_quarter], gate_up[:, hidden_quarter:]
    sig = jax.nn.sigmoid(gate)
    hidden = (gate * sig * upward).astype(bf16)
    grad_gate = grad_hidden * upward * sig * (1.0 + gate * (1.0 - sig))
    grad_gate_up = jnp.concatenate([grad_gate.astype(bf16), (grad_hidden * gate * sig).astype(bf16)], axis=1)
    partial, carried = both(dot_nt(grad_gate_up, w_feed), carried)
    blocks, carried, grad_gate_up, hidden = both(scatter_half(partial), carried, grad_gate_up, hidden)
    mine_two = jnp.concatenate([block[:, :D] for block in carried], axis=0)
    att_quarter = carried
    grad_three, grad_feed, full_two = both(
        scatter_x(blocks), products((full_three, grad_gate_up), (full_grad, hidden)), with_partner(mine_two)
    )
    sum_feed = scatter_plane(grad_feed)
    grad_resid_two = upstream.astype(f32) + unit_norm_back(norm_three, scale_three, summed(grad_three))

    sent_two = grad_resid_two.astype(bf16)
    mine_two = gather_half(sent_two)
    pair_grad = pair_rows(sent_two)
    grad_cross_att = dot(pair_grad, w_co).astype(bf16)
    grad_cq, quarters = cross_backward(scalars, cross_q, cond_kv, bias, grad_cross_att)
    grad_cq, mine_two = both(grad_cq, mine_two)
    grad_two = pair_sum(dot_nt(grad_cq, w_cq))
    grad_resid_one = grad_resid_two + unit_norm_back(norm_two, scale_two, grad_two)

    sent_back, mine_two, quarters, hidden = both(grad_resid_one.astype(bf16), mine_two, quarters, hidden)
    mine_back, grad_two_all, hidden = both(gather_half(sent_back), with_partner(mine_two), hidden)
    full_back, quarters, feed_part = both(with_partner(mine_back), quarters, dot_nt(hidden, w_down).astype(bf16))
    grad_att, quarters, feed_part = both(dot(full_back, w_out).astype(bf16), quarters, feed_part)
    feed_half = scatter_half(feed_part)
    quarter_parts = swapped_x([quarters[k] for k in range(4)])
    feed_parts = scatter_x(feed_half)
    grad_qvk = attn_backward(qs, ks, vs, grad_att, lse, cosine, sine)
    grad_qvk, quarter_parts, sum_feed = both(grad_qvk, quarter_parts, sum_feed)
    ckv_share = summed([part[ROWS:] for part in quarter_parts]).astype(bf16)
    grad_attn, grad_qvk, ckv_share, sum_feed, sum_feed_far, feed_near = both(
        attn_products(
            full_one, grad_qvk, full_back, attended, own_context, ckv_share, full_two, grad_two_all, quarter_parts, att_quarter
        ),
        grad_qvk,
        ckv_share,
        sum_feed,
        to_far(sum_feed),
        gather_x(sum_feed),
    )
    parts_attn = plane_parts(grad_attn)
    half = 4 * ROWS
    blocks = halves_sum(dot_nt(grad_qvk[:half], w_qvk), dot_nt(grad_qvk[half:], w_qvk).astype(bf16))
    blocks, ckv_share, sum_feed_far, feed_near = both(blocks, ckv_share, sum_feed_far, feed_near)
    feed_all = [*feed_near, *gather_x(sum_feed_far)]
    cond_part = dot_nt(ckv_share, w_kv)[:cond_count]
    cond_part = (cond_part + to_partner(cond_part)).astype(bf16)
    grad_one, feed_parts = both(scatter_x(blocks), feed_parts)
    feed_branch = summed(feed_parts)
    output = resid_two + feed_branch
    sent_out = permuted(output.astype(bf16))
    in_grad = grad_resid_one + unit_norm_back(norm_one, scale_one, summed(grad_one))

    def columns_of(back):
        return lax.dynamic_slice_in_dim(cond_part, (x + 4 - back) % 4 * (D // 4), D // 4, 1)

    cond_parts = scatter_x([columns_of(back) for back in range(4)])
    cond_near = jnp.stack(gather_x(permuted(summed(cond_parts).astype(bf16))))
    at = jnp.stack([x, yh]).astype(jnp.int32)

    def column(gain):
        return gain.astype(f32)[:, None]

    grad_feed_in, grad_feed_out = finish_feed(at, feed_all, column(gain_feed))

    def row_sums(w, grad):
        sums = jnp.sum(w.astype(f32) * grad.astype(f32), axis=1)
        return jnp.pad(sums, (0, 128 - half_rows))

    row = jnp.arange(own_rows, dtype=jnp.int32)
    valid = ((2 * x + tp) * own_rows + row < length)[:, None]
    squares = [jnp.sum(jnp.where(valid, v * v, 0.0)) for v in (tokens, attn_branch, cross_branch, feed_branch, output)]
    small = jnp.concatenate([row_sums(feed_cols, sum_feed[:, : 2 * hidden_quarter]), jnp.pad(jnp.stack(squares), (0, 123))])

    moved_in = lax.ppermute(permuted(in_grad.astype(bf16)), ("yh", "tp"), SWAP)
    moved_out = lax.ppermute(sent_out, ("yh", "tp"), SWAP)
    parts_attn, moved_in, moved_out, small, grad_feed_in, grad_feed_out = both(
        parts_attn, moved_in, moved_out, small, grad_feed_in, grad_feed_out
    )
    sum_attn = total(parts_attn)
    attn_own, cond_near = both(sum_attn.astype(bf16), cond_near)
    attn_near, attn_far, sum_attn, small, moved_in, moved_out, cond_near = both(
        gather_x(attn_own), to_far(attn_own), sum_attn, small, moved_in, moved_out, cond_near
    )
    attn_all = [*attn_near, *gather_x(attn_far)]
    more = [row_sums(qvk_cols, sum_attn[:, : 3 * quarter])]
    more += [row_sums(own_cols(cq_half, quarter), sum_attn[:, 6 * quarter : 7 * quarter])]
    small = sent_to_all(jnp.concatenate([*more, small])[None], ("x", "yh", "tp"), 16).reshape(4, 2, 2, 4, 128)
    in_grad = lax.all_gather(moved_in, "tp", axis=0, tiled=False).astype(f32)
    layer_out = lax.all_gather(moved_out, "tp", axis=0, tiled=False)
    cond_grad = finish_cond(at, cond_near, to_far(cond_near)).transpose(1, 0, 2)
    proj, out, keyval, query, cross = finish_columns(at, attn_all, column(gain_attn), column(gain_cross))
    small = jnp.sum(small, axis=(0, 2))
    layer_stats = jnp.sqrt(small[:, 3, :5] / (lengths.astype(f32)[:, None] * D))
    gains = [small[:, k, :half_rows].reshape(2 * half_rows) for k in range(3)]

    return (
        layer_out,
        in_grad,
        cond_grad,
        layer_stats,
        gains[0],
        proj.transpose(1, 0, 2),
        out,
        gains[1],
        query,
        keyval,
        cross,
        gains[2],
        grad_feed_in,
        grad_feed_out,
    )


def solution(mesh):
    fine = Mesh(mesh.devices.reshape(4, 2, 4, 2, 2), ("z", "yl", "x", "yh", "tp"))
    weights = (
        P(DP),
        P(DP, None, "tp"),
        P(DP, "tp"),
        P(DP),
        P(DP, "tp"),
        P(DP, None, "tp"),
        P(DP, "tp"),
        P(DP),
        P(DP, None, "tp"),
        P(DP, "tp"),
    )
    return jax.shard_map(
        per_device,
        mesh=fine,
        in_specs=(P(DP, CTX, None), P(DP, None, None), P(DP), P(DP, None), P(DP, CTX, None), *weights),
        out_specs=(P(DP, CTX, None), P(DP, CTX, None), P(DP, None, None), P(DP, None), *weights),
        check_vma=False,
    )
```

```python
import jax
import jax.numpy as jnp
from jax import lax
from jax.experimental import pallas as pl
from jax.experimental.pallas import tpu as pltpu
from jax.sharding import Mesh
from jax.sharding import PartitionSpec as P

DP = ("z", "yl")
CTX = ("x", "yh")
PLANE = ("z", "yh", "yl")
SWAP = ((0, 0), (1, 2), (2, 1), (3, 3))

D = 1536
HD = 64
ROT = 32
HEADS = 3
WIDE = 256
V_AT, K_AT, O_AT, QVK = 128, 384, 512, 640
ROWS = 128
SEQ = 1024
QB = 256
CROSS_KEYS = 144
norm_eps = 1e-05
masked_fill = -1e30
bf16 = jnp.bfloat16
f32 = jnp.float32


def permuted(v):
    parts = []
    for z in range(v.shape[-1] // 384):
        for piece in (0, 2, 1, 3):
            at = z * 384 + piece * 96
            parts.append(v[..., at : at + 96])
    return jnp.concatenate(parts, axis=-1)


def dot(a, b):
    return jnp.dot(a, b, preferred_element_type=f32)


def dot_nt(a, b):
    return lax.dot_general(a, b, (((1,), (1,)), ((), ())), preferred_element_type=f32)


def dot_tn(a, b):
    return lax.dot_general(a, b, (((0,), (0,)), ((), ())), preferred_element_type=f32)


def to_partner(v):
    return lax.ppermute(v, "tp", ((0, 1), (1, 0)))


def exchanged(v, axes):
    return lax.all_to_all(v, axes, split_axis=0, concat_axis=0, tiled=True)


def sent_to_all(v, axes, count):
    return exchanged(jnp.broadcast_to(v[None], (count, *v.shape)), axes)


def after(values, *others):
    return lax.optimization_barrier((values, others))[0]


def both(first, *others):
    return lax.optimization_barrier((first, *others))


def along_x(v, step):
    return lax.ppermute(v, "x", [(i, (i + step) % 4) for i in range(4)])


def gather_x(own):
    return [own] + [along_x(own, step) for step in (1, 2, 3)]


def scatter_x(blocks):
    return [blocks[0]] + [along_x(blocks[step], -step) for step in (1, 2, 3)]


def swapped_x(blocks):
    return [blocks[0]] + [along_x(blocks[step], step) for step in (1, 2, 3)]


def summed(blocks):
    return sum(block.astype(f32) for block in blocks[1:]) + blocks[0].astype(f32)


def gather_half(own):
    return jnp.concatenate(gather_x(own), axis=0)


def to_far(v):
    return lax.ppermute(v, "yh", ((0, 1), (1, 0)))


def with_partner(mine):
    return jnp.concatenate([mine, to_partner(mine)], axis=0)


def halves_sum(near, far):
    mine = (near.astype(f32) + to_partner(far).astype(f32)).astype(bf16)
    return [mine[k * ROWS : (k + 1) * ROWS] for k in range(4)]


def scatter_half(partial):
    half = 4 * ROWS
    return halves_sum(partial[:half], partial[half:].astype(bf16))


def plane_parts(grad):
    return exchanged(grad.astype(bf16).reshape(16, grad.shape[0] // 16, grad.shape[1]), PLANE)


def total(parts):
    return jnp.sum(parts.astype(f32), axis=0)


def pair_rows(own):
    return jnp.concatenate([own, to_partner(own)], axis=0)


def pair_sum(partial):
    return partial[:ROWS] + to_partner(partial[ROWS:])


def gather_plane(shard):
    return lax.all_gather(shard, PLANE, axis=0, tiled=True)


def scatter_plane(grad):
    return lax.psum_scatter(grad, PLANE, scatter_dimension=0, tiled=True)


def unit_norm(v):
    centered = v - jnp.mean(v, axis=-1, keepdims=True)
    scale = lax.rsqrt(jnp.mean(centered * centered, axis=-1, keepdims=True) + norm_eps)
    return centered * scale, scale


def unit_norm_back(x_hat, scale, grad):
    along = jnp.mean(grad * x_hat, axis=-1, keepdims=True)
    return scale * (grad - jnp.mean(grad, axis=-1, keepdims=True) - x_hat * along)


def lane_masks(rows):
    lane = lax.broadcasted_iota(jnp.int32, (rows, WIDE), 1)
    heads = [(lane // HD == h).astype(f32).astype(bf16) for h in range(HEADS + 1)]
    return lane, heads, (lane == HEADS * HD).astype(f32).astype(bf16)


def turned(v, cosine, sine, first):
    other = jnp.where(first, pltpu.roll(v, WIDE - ROT // 2, 1), pltpu.roll(v, ROT // 2, 1))
    cosine, sine = (jnp.concatenate([table, table], axis=1) for table in (cosine, sine))
    return v * cosine, other * sine


def attn_forward_kernel(sc, qkv, cosine, sine, att, qs, ks, vs, lse, vt):
    lane, heads, extra = lane_masks(QB)
    first = lane % HD < ROT // 2
    value_head = lax.broadcasted_iota(jnp.int32, (WIDE, QB), 0) // HD - 1

    def prepare(block, carry):
        rows = pl.ds(block * QB, QB)
        c, s = cosine[rows, :], sine[rows, :]
        straight, crossed = turned(qkv[rows, 0:WIDE], c, s, first)
        query = ((straight + crossed) * HD ** (-0.5)).astype(bf16)
        qs[rows, :] = jnp.where(lane < HEADS * HD, query.astype(f32), jnp.where(lane == HEADS * HD, 1.0, 0.0)).astype(bf16)
        straight, crossed = turned(qkv[rows, K_AT : K_AT + WIDE], c, s, first)
        row = lax.broadcasted_iota(jnp.int32, (QB, WIDE), 0) + block * QB
        side = jnp.where(row < SEQ // 2, sc[0], 1 - sc[0])
        within = row % (SEQ // 2)
        place = ((sc[2] + 4 - within // ROWS) % 4 * 2 + side) * ROWS + within % ROWS
        fill = jnp.where((lane == HEADS * HD) & (place >= sc[1]), masked_fill, 0.0)
        ks[rows, :] = jnp.where(lane < HEADS * HD, straight + crossed, fill).astype(bf16)
        value = qkv[rows, V_AT : V_AT + WIDE]
        vs[rows, :] = value.astype(bf16)
        vt[:, rows] = value.T.astype(bf16)
        return carry

    for block in range(SEQ // QB):
        prepare(block, 0)

    def attend(block, carry):
        rows = pl.ds(pl.multiple_of(block * QB, QB), QB)
        query = qs[rows, :]
        total = jnp.zeros((WIDE, QB), f32)
        for h in range(HEADS):
            scores = dot_nt(ks[...], query * (heads[h] + extra))
            top = jnp.max(scores, axis=0, keepdims=True)
            weight = jnp.exp(scores - top)
            mass = jnp.sum(weight, axis=0, keepdims=True)
            out = dot(vt[...], weight.astype(bf16))
            total = jnp.where(value_head == h, out / mass, total)
            lse[h : h + 1, rows] = top + jnp.log(mass)
        att[rows, :] = total.T.astype(bf16)
        return carry

    lse[...] = jnp.zeros(lse.shape, f32)
    lax.fori_loop(0, SEQ // QB, attend, 0)


def attn_forward(scalars, qkv, cosine, sine):
    wide = jax.ShapeDtypeStruct((SEQ, WIDE), bf16)
    return pl.pallas_call(
        attn_forward_kernel,
        in_specs=[pl.BlockSpec(memory_space=pltpu.SMEM)] + [pl.BlockSpec(memory_space=pltpu.VMEM)] * 3,
        out_shape=(wide, wide, wide, wide, jax.ShapeDtypeStruct((8, SEQ), f32)),
        scratch_shapes=[pltpu.VMEM((WIDE, SEQ), bf16)],
        cost_estimate=pl.CostEstimate(flops=4 * HEADS * SEQ * SEQ * WIDE, transcendentals=HEADS * SEQ * SEQ, bytes_accessed=8 << 20),
    )(scalars, qkv, cosine, sine)


def attn_backward_kernel(qs, ks, vs, grad, lse, cosine, sine, out, kt, dq, dk, dv):
    lane, heads, extra = lane_masks(QB)
    first = lane % HD < ROT // 2
    wide_head = lax.broadcasted_iota(jnp.int32, (WIDE, QB), 0) // HD
    kept = lane < HEADS * HD
    kt[...] = ks[...].astype(f32).T.astype(bf16)
    dk[...] = jnp.zeros(dk.shape, f32)
    dv[...] = jnp.zeros(dv.shape, f32)

    def step(block, carry):
        rows = pl.ds(pl.multiple_of(block * QB, QB), QB)
        query, given = qs[rows, :], grad[rows, :]
        total = jnp.zeros((WIDE, QB), f32)
        for h in range(HEADS):
            own_query, own_grad = query * heads[h], given * heads[h + 1]
            scores = dot_nt(ks[...], query * (heads[h] + extra))
            weight = jnp.exp(scores - lse[h : h + 1, rows])
            wanted = dot_nt(vs[...], own_grad)
            product = weight * wanted
            inner = jnp.sum(product, axis=0, keepdims=True)
            slope = (product - weight * inner).astype(bf16)
            dv[...] += dot(weight.astype(bf16), own_grad)
            dk[...] += dot(slope, own_query)
            total = jnp.where(wide_head == h, dot(kt[...], slope), total)
        straight, crossed = turned(total.T * HD ** (-0.5), cosine[rows, :], sine[rows, :], first)
        turned_back = straight - crossed
        out[rows, 0:128] = turned_back[:, :128].astype(bf16)
        dq[rows, :] = turned_back[:, 128:]
        return carry

    lax.fori_loop(0, SEQ // QB, step, 0)
    for block in range(SEQ // QB):
        rows = pl.ds(block * QB, QB)
        value = dv[rows, :]
        out[rows, V_AT : V_AT + 128] = jnp.where(lane[:, :128] < HD, dq[rows, :], value[:, :128]).astype(bf16)
        out[rows, V_AT + 128 : V_AT + 256] = value[:, 128:].astype(bf16)
        straight, crossed = turned(dk[rows, :], cosine[rows, :], sine[rows, :], first)
        out[rows, K_AT : K_AT + WIDE] = jnp.where(kept, straight - crossed, 0.0).astype(bf16)


def attn_backward(qs, ks, vs, grad, lse, cosine, sine):
    return pl.pallas_call(
        attn_backward_kernel,
        in_specs=[pl.BlockSpec(memory_space=pltpu.VMEM)] * 7,
        out_shape=jax.ShapeDtypeStruct((SEQ, QVK), bf16),
        scratch_shapes=[pltpu.VMEM((WIDE, SEQ), bf16), pltpu.VMEM((SEQ, 128), f32), pltpu.VMEM((SEQ, WIDE), f32), pltpu.VMEM((SEQ, WIDE), f32)],
        cost_estimate=pl.CostEstimate(flops=10 * HEADS * SEQ * SEQ * WIDE, transcendentals=HEADS * SEQ * SEQ, bytes_accessed=8 << 20),
    )(qs, ks, vs, grad, lse, cosine, sine)


PAIR = 2 * HD
QUARTER = HEADS * HD


def pair_of(sc, kv, group, kind):
    lanes = []
    for head in (2 * group, 2 * group + 1):
        at = kind * QUARTER + head % HEADS * HD
        lanes.append(kv[(sc[2] + 4 - head // HEADS) % 4, :, at : at + HD])
    return jnp.concatenate(lanes, axis=1)


def cross_weights(query, keys, bias):
    scores = dot_nt(keys, query) + bias
    weight = jnp.exp(scores - jnp.max(scores, axis=0, keepdims=True))
    return weight / jnp.sum(weight, axis=0, keepdims=True)


def store_quarters(sc, out, group, value):
    for h in range(2):
        head = 2 * group + h
        at = head % HEADS * HD
        for side in range(2):
            piece = value[side * ROWS : (side + 1) * ROWS, h * HD : (h + 1) * HD]
            out[(head // HEADS + 4 - sc[2]) % 4, 0:ROWS, side * QUARTER + at : side * QUARTER + at + HD] = piece


def cross_forward_kernel(sc, cq, kv, bias, att, quarters):
    lane = lax.broadcasted_iota(jnp.int32, (2 * ROWS, PAIR), 1)
    row = lax.broadcasted_iota(jnp.int32, (PAIR, 2 * ROWS), 0)
    for group in range(cq.shape[1] // PAIR):
        at = pl.ds(group * PAIR, PAIR)
        query, keys = cq[:, at], pair_of(sc, kv, group, 0)
        values = pair_of(sc, kv, group, 1).astype(f32).T.astype(bf16)
        outs = []
        for h in range(2):
            mask = (lane // HD == h).astype(f32).astype(bf16)
            weight = cross_weights(query * mask, keys, bias[...])
            outs.append(dot(values, weight.astype(bf16)))
        value = jnp.where(row < HD, outs[0], outs[1]).T.astype(bf16)
        att[:, at] = value
        store_quarters(sc, quarters, group, value)


def cross_forward(scalars, cq, kv, bias):
    return pl.pallas_call(
        cross_forward_kernel,
        in_specs=[pl.BlockSpec(memory_space=pltpu.SMEM)] + [pl.BlockSpec(memory_space=pltpu.VMEM)] * 3,
        out_shape=(jax.ShapeDtypeStruct(cq.shape, bf16), jax.ShapeDtypeStruct((4, ROWS, 2 * QUARTER), bf16)),
        cost_estimate=pl.CostEstimate(flops=4 * 12 * 256 * 144 * 128, transcendentals=12 * 256 * 144, bytes_accessed=2 << 20),
    )(scalars, cq, kv, bias)


def cross_backward_kernel(sc, cq, kv, bias, grad, dq, quarters):
    lane = lax.broadcasted_iota(jnp.int32, (2 * ROWS, PAIR), 1)
    row = lax.broadcasted_iota(jnp.int32, (PAIR, 2 * ROWS), 0)
    for group in range(cq.shape[1] // PAIR):
        at = pl.ds(group * PAIR, PAIR)
        query, given = cq[:, at], grad[:, at]
        keys, values = pair_of(sc, kv, group, 0), pair_of(sc, kv, group, 1)
        turned_keys = keys.astype(f32).T.astype(bf16)
        outs, grads = [], [0.0, 0.0]
        for h in range(2):
            mask = (lane // HD == h).astype(f32).astype(bf16)
            own_query, own_grad = query * mask, given * mask
            weight = cross_weights(own_query, keys, bias[...])
            product = weight * dot_nt(values, own_grad)
            slope = (product - weight * jnp.sum(product, axis=0, keepdims=True)).astype(bf16)
            outs.append(dot(turned_keys, slope))
            grads[0] += dot(slope, own_query)
            grads[1] += dot(weight.astype(bf16), own_grad)
        value = (jnp.where(row < HD, outs[0], outs[1]).T * HD ** (-0.5)).astype(bf16)
        dq[:, at] = value
        store_quarters(sc, quarters, group, value)
        for h in range(2):
            head = 2 * group + h
            for kind in range(2):
                place = kind * QUARTER + head % HEADS * HD
                piece = grads[kind][:, h * HD : (h + 1) * HD].astype(bf16)
                quarters[(head // HEADS + 4 - sc[2]) % 4, ROWS:, place : place + HD] = piece


def cross_backward(scalars, cq, kv, bias, grad):
    return pl.pallas_call(
        cross_backward_kernel,
        in_specs=[pl.BlockSpec(memory_space=pltpu.SMEM)] + [pl.BlockSpec(memory_space=pltpu.VMEM)] * 4,
        out_shape=(
            jax.ShapeDtypeStruct(cq.shape, bf16),
            jax.ShapeDtypeStruct((4, ROWS + kv.shape[1], 2 * QUARTER), bf16),
        ),
        cost_estimate=pl.CostEstimate(flops=10 * 12 * 256 * 144 * 128, transcendentals=12 * 256 * 144, bytes_accessed=3 << 20),
    )(scalars, cq, kv, bias, grad)


def rotary_lanes(side, x):
    row = jnp.arange(SEQ, dtype=jnp.int32)
    within = row % (SEQ // 2)
    part = jnp.where(row < SEQ // 2, side, 1 - side)
    place = (((x + 4 - within // ROWS) % 4 * 2 + part) * ROWS + within % ROWS).astype(f32)
    lane = jnp.arange(128, dtype=jnp.int32) % HD
    exponent = (lane % (ROT // 2)).astype(f32) * (2.0 / ROT)
    angle = place[:, None] * jnp.power(jnp.float32(10000.0), -exponent)[None, :]
    inside = (lane < ROT)[None, :]
    sign = jnp.where(lane < ROT // 2, -1.0, 1.0)[None, :]
    return jnp.where(inside, jnp.cos(angle), 1.0), jnp.where(inside, jnp.sin(angle) * sign, 0.0)


def products_kernel(count, *refs):
    out, at = refs[-1], 0
    for k in range(count):
        left, right = refs[2 * k], refs[2 * k + 1]
        width = right.shape[1]
        out[:, at : at + width] = dot_tn(left[...], right[...]).astype(bf16)
        at += width


def products(*pairs):
    tile, total_width = 256, sum(right.shape[1] for _, right in pairs)
    flat, specs = [], []
    for left, right in pairs:
        flat += [left, right]
        specs += [pl.BlockSpec((left.shape[0], tile), lambda i: (0, i)), pl.BlockSpec(right.shape, lambda i: (0, 0))]
    work = sum(left.shape[0] * right.shape[1] for left, right in pairs)
    return pl.pallas_call(
        lambda *refs: products_kernel(len(pairs), *refs),
        grid=(D // tile,),
        in_specs=specs,
        out_specs=pl.BlockSpec((tile, total_width), lambda i: (i, 0)),
        out_shape=jax.ShapeDtypeStruct((D, total_width), bf16),
        cost_estimate=pl.CostEstimate(flops=2 * D * work, transcendentals=0, bytes_accessed=10 << 20),
    )(*flat)


def by_rows(blocks, at):
    starts = (at, at + QUARTER)
    return jnp.concatenate([b[:ROWS, k : k + QUARTER] for k in starts for b in blocks], axis=0)


def attn_products_kernel(one, grad, back, att, context, share, two, three, *rest):
    cq, catt, out = rest[:4], rest[4:8], rest[8]
    proj, across = dot_tn(one[...], grad[...]), dot_tn(back[...], att[...])
    out[:, :O_AT] = proj[:, :O_AT].astype(bf16)
    out[:, O_AT:QVK] = (proj[:, O_AT:] + across[:, : QVK - O_AT]).astype(bf16)
    out[:, QVK : O_AT + WIDE] = across[:, QVK - O_AT :].astype(bf16)
    at = O_AT + WIDE
    out[:, at : at + 2 * QUARTER] = dot_tn(context[...], share[...]).astype(bf16)
    at += 2 * QUARTER
    pieces = [dot_tn(two[...], by_rows(cq, 0)).astype(bf16), dot_tn(three[...], by_rows(catt, D)).astype(bf16)]
    out[:, at:] = jnp.concatenate(pieces, axis=1)


def attn_products(one, grad, back, att, context, share, two, three, cq, catt):
    tile, width = 256, O_AT + WIDE + 4 * QUARTER

    def whole(v):
        return pl.BlockSpec(v.shape, lambda i: (0, 0))

    def piece(v):
        return pl.BlockSpec((v.shape[0], tile), lambda i: (0, i))

    specs = [piece(one), whole(grad), piece(back), whole(att), piece(context), whole(share), piece(two), piece(three)]
    return pl.pallas_call(
        attn_products_kernel,
        grid=(D // tile,),
        in_specs=specs + [whole(v) for v in (*cq, *catt)],
        out_specs=pl.BlockSpec((tile, width), lambda i: (i, 0)),
        out_shape=jax.ShapeDtypeStruct((D, width), bf16),
        cost_estimate=pl.CostEstimate(flops=2 * D * SEQ * width, transcendentals=0, bytes_accessed=16 << 20),
    )(one, grad, back, att, context, share, two, three, *cq, *catt)


def held_at(q, x):
    return (x + 4 - q) % 4


def finish_feed_kernel(at, *refs):
    blocks, (gain, grad_in, grad_down, held) = refs[:8], refs[8:]
    rows, width = blocks[0].shape[0], grad_down.shape[1] // 4
    for k, block in enumerate(blocks):
        held[k % 4, k // 4] = block[...]
    for h in range(2):
        scale = gain[h * rows : (h + 1) * rows, :]
        for q in range(4):
            part = held[held_at(q, at[0]), (at[1] + h) % 2]
            to = pl.ds(q * width, width)
            for kind in range(2):
                grad_in[h * rows : (h + 1) * rows, kind, to] = part[:, kind * width : (kind + 1) * width].astype(f32) * scale
            grad_down[h * rows : (h + 1) * rows, to] = part[:, 2 * width :].astype(f32)


def finish_feed(at, blocks, gain):
    rows, columns = blocks[0].shape
    width = columns // 3
    return pl.pallas_call(
        finish_feed_kernel,
        in_specs=[pl.BlockSpec(memory_space=pltpu.SMEM)] + [pl.BlockSpec(memory_space=pltpu.VMEM)] * 9,
        out_shape=(
            jax.ShapeDtypeStruct((2 * rows, 2, 4 * width), f32),
            jax.ShapeDtypeStruct((2 * rows, 4 * width), f32),
        ),
        scratch_shapes=[pltpu.VMEM((4, 2, rows, columns), bf16)],
        cost_estimate=pl.CostEstimate(flops=1 << 22, transcendentals=0, bytes_accessed=11 << 20),
    )(at, *blocks, gain)


def finish_cond_kernel(at, near, far, out):
    width = near.shape[2]
    for q in range(4):
        place = held_at(q, at[0])
        near_block, far_block = near[place].astype(f32), far[place].astype(f32)
        for h in range(2):
            out[:, h, q * width : (q + 1) * width] = jnp.where(at[1] == h, near_block, far_block)


def finish_cond(at, near, far):
    _, count, width = near.shape
    return pl.pallas_call(
        finish_cond_kernel,
        in_specs=[pl.BlockSpec(memory_space=pltpu.SMEM)] + [pl.BlockSpec(memory_space=pltpu.VMEM)] * 2,
        out_shape=jax.ShapeDtypeStruct((count, 2, 4 * width), f32),
        cost_estimate=pl.CostEstimate(flops=1 << 20, transcendentals=0, bytes_accessed=3 << 20),
    )(at, near, far)


def finish_columns_kernel(at, *refs):
    blocks, (gain, other_gain, proj, out, keyval, query, cross, held) = refs[:8], refs[8:]
    rows = blocks[0].shape[0]
    for k, block in enumerate(blocks):
        held[k % 4, k // 4] = block[...]
    for h in range(2):
        to = pl.ds(h * rows, rows)
        parts = [held[held_at(q, at[0]), (at[1] + h) % 2] for q in range(4)]

        def kind_of(kind):
            row = [part[:, kind * QUARTER : (kind + 1) * QUARTER].astype(f32) for part in parts]
            return jnp.concatenate(row, axis=1)

        for place, kind in enumerate((0, 2, 1)):
            proj[place, to, :] = kind_of(kind) * gain[to, :]
        out[to, :] = kind_of(3)
        keyval[to, 0, :] = kind_of(4)
        keyval[to, 1, :] = kind_of(5)
        query[to, :] = kind_of(6) * other_gain[to, :]
        cross[to, :] = kind_of(7)


def finish_columns(at, blocks, gain, other_gain):
    rows, columns = blocks[0].shape
    width = columns // 2
    plain = jax.ShapeDtypeStruct((2 * rows, width), f32)
    return pl.pallas_call(
        finish_columns_kernel,
        in_specs=[pl.BlockSpec(memory_space=pltpu.SMEM)] + [pl.BlockSpec(memory_space=pltpu.VMEM)] * 10,
        out_shape=(
            jax.ShapeDtypeStruct((3, 2 * rows, width), f32),
            plain,
            jax.ShapeDtypeStruct((2 * rows, 2, width), f32),
            plain,
            plain,
        ),
        scratch_shapes=[pltpu.VMEM((4, 2, rows, columns), bf16)],
        cost_estimate=pl.CostEstimate(flops=1 << 20, transcendentals=0, bytes_accessed=4 << 20),
    )(at, *blocks, gain, other_gain)


def per_device(
    hidden_in,
    context,
    lengths,
    cond_mask,
    out_grad,
    gain_attn,
    self_proj,
    self_out,
    gain_cross,
    cross_query,
    cross_keyval,
    cross_out,
    gain_feed,
    feed_in,
    feed_out,
):
    x, yh, tp = lax.axis_index("x"), lax.axis_index("yh"), lax.axis_index("tp")
    cond_count = context.shape[1]
    own_rows = hidden_in.shape[1]
    half_rows = self_proj.shape[0] // 2
    quarter = self_proj.shape[2] // 4
    hidden_quarter = feed_in.shape[2] // 4
    local_width = self_proj.shape[2]

    def own_half(w):
        return lax.dynamic_slice_in_dim(w, yh * half_rows, half_rows, 0)

    def own_cols(w, count):
        return lax.dynamic_slice_in_dim(w, x * count, count, w.ndim - 1)

    def scaled(w, gain):
        return (w.astype(f32) * own_half(gain).astype(f32)[:, None]).astype(bf16)

    x_own = lax.ppermute(lax.dynamic_index_in_dim(hidden_in, tp, 0, False), ("yh", "tp"), SWAP)
    u_own = lax.ppermute(lax.dynamic_index_in_dim(out_grad, tp, 0, False), ("yh", "tp"), SWAP)
    length = lax.dynamic_index_in_dim(lengths, yh, 0, False)
    own_mask = lax.dynamic_index_in_dim(cond_mask, yh, 0, False)
    tokens = permuted(x_own).astype(f32)
    norm_one, scale_one = unit_norm(tokens)

    qkv_cols = own_cols(own_half(self_proj), quarter)
    qvk_cols = jnp.concatenate([qkv_cols[:, 0], qkv_cols[:, 2], qkv_cols[:, 1]], axis=1)
    out_cols = own_cols(own_half(self_out), quarter)
    keyval_cols = own_cols(own_half(cross_keyval), quarter).reshape(half_rows, 2 * quarter)
    cq_half = own_half(cross_query)
    first_set = gather_plane(
        jnp.concatenate([scaled(qvk_cols, gain_attn), out_cols, keyval_cols, scaled(cq_half, gain_cross), own_half(cross_out)], axis=1)
    )
    sent_one = norm_one.astype(bf16)
    sent_one, feed_in, feed_out, context = both(sent_one, feed_in, feed_out, context)
    feed_cols = own_cols(own_half(feed_in), hidden_quarter).reshape(half_rows, 2 * hidden_quarter)
    down_cols = own_cols(own_half(feed_out), hidden_quarter)
    feed_set = gather_plane(jnp.concatenate([scaled(feed_cols, gain_feed), down_cols], axis=1))
    w_qvk, w_out = first_set[:, :QVK], first_set[:, O_AT : O_AT + WIDE]
    cq_at = O_AT + WIDE + 2 * quarter
    w_kv, w_cq, w_co = first_set[:, O_AT + WIDE : cq_at], first_set[:, cq_at : cq_at + local_width], first_set[:, cq_at + local_width :]
    w_feed, w_down = feed_set[:, : 2 * hidden_quarter], feed_set[:, 2 * hidden_quarter :]

    scalars = jnp.stack([tp.astype(jnp.int32), length, x.astype(jnp.int32)])
    own_context = jnp.pad(lax.dynamic_index_in_dim(context, yh, 0, False), ((0, CROSS_KEYS - cond_count), (0, 0)))
    mine_one, u_own, cosine, sine, own_context = both(
        gather_half(sent_one), u_own, *rotary_lanes(tp, x), permuted(own_context)
    )
    upstream = permuted(u_own)
    full_one, mine_grad = both(with_partner(mine_one), gather_half(upstream))
    qvk, keyval, full_grad = both(dot(full_one, w_qvk), dot(own_context, w_kv).astype(bf16), with_partner(mine_grad))
    attended, qs, ks, vs, lse = attn_forward(scalars, qvk, cosine, sine)
    attended, keyval = both(attended, gather_x(keyval))
    cond_kv = jnp.stack(keyval)
    blocks = both(*scatter_half(dot_nt(attended, w_out)))
    attn_branch = summed(both(*scatter_x(blocks)))
    resid_one = tokens + attn_branch

    seen = jnp.pad(own_mask > 0, (0, CROSS_KEYS - cond_count))
    bias = jnp.broadcast_to(jnp.where(seen, 0.0, masked_fill)[:, None], (CROSS_KEYS, 2 * own_rows)).astype(f32)
    norm_two, scale_two = unit_norm(resid_one)
    sent_two = norm_two.astype(bf16)
    pair_two = pair_rows(sent_two)
    cross_q = (dot(pair_two, w_cq) * HD ** (-0.5)).astype(bf16)
    cross_att, att_quarters = cross_forward(scalars, cross_q, cond_kv, bias)
    cross_branch = pair_sum(dot_nt(cross_att, w_co))
    resid_two = resid_one + cross_branch
    norm_three, scale_three = unit_norm(resid_two)

    sent_three, full_grad, sent_two, att_quarters = both(norm_three.astype(bf16), full_grad, sent_two, att_quarters)
    mine_three, grad_hidden = both(gather_half(sent_three), dot(full_grad, w_down))
    full_three, sent_two, att_quarters = both(with_partner(mine_three), sent_two, att_quarters)
    carried = [jnp.concatenate([sent_two, att_quarters[k]], axis=1) for k in range(4)]
    carried = swapped_x(carried)
    gate_up = dot(full_three, w_feed)
    gate, upward = gate_up[:, :hidden_quarter], gate_up[:, hidden_quarter:]
    sig = jax.nn.sigmoid(gate)
    hidden = (gate * sig * upward).astype(bf16)
    grad_gate = grad_hidden * upward * sig * (1.0 + gate * (1.0 - sig))
    grad_gate_up = jnp.concatenate([grad_gate.astype(bf16), (grad_hidden * gate * sig).astype(bf16)], axis=1)
    partial, carried = both(dot_nt(grad_gate_up, w_feed), carried)
    blocks, carried, grad_gate_up, hidden = both(scatter_half(partial), carried, grad_gate_up, hidden)
    mine_two = jnp.concatenate([block[:, :D] for block in carried], axis=0)
    att_quarter = carried
    grad_three, grad_feed, full_two = both(
        scatter_x(blocks), products((full_three, grad_gate_up), (full_grad, hidden)), with_partner(mine_two)
    )
    sum_feed = scatter_plane(grad_feed)
    grad_resid_two = upstream.astype(f32) + unit_norm_back(norm_three, scale_three, summed(grad_three))

    sent_two = grad_resid_two.astype(bf16)
    mine_two = gather_half(sent_two)
    pair_grad = pair_rows(sent_two)
    grad_cross_att = dot(pair_grad, w_co).astype(bf16)
    grad_cq, quarters = cross_backward(scalars, cross_q, cond_kv, bias, grad_cross_att)
    grad_cq, mine_two = both(grad_cq, mine_two)
    grad_two = pair_sum(dot_nt(grad_cq, w_cq))
    grad_resid_one = grad_resid_two + unit_norm_back(norm_two, scale_two, grad_two)

    sent_back, mine_two, quarters, hidden = both(grad_resid_one.astype(bf16), mine_two, quarters, hidden)
    mine_back, grad_two_all, hidden = both(gather_half(sent_back), with_partner(mine_two), hidden)
    full_back, quarters, feed_part = both(with_partner(mine_back), quarters, dot_nt(hidden, w_down).astype(bf16))
    grad_att, quarters, feed_part = both(dot(full_back, w_out).astype(bf16), quarters, feed_part)
    feed_half = scatter_half(feed_part)
    quarter_parts = swapped_x([quarters[k] for k in range(4)])
    feed_parts = scatter_x(feed_half)
    grad_qvk = attn_backward(qs, ks, vs, grad_att, lse, cosine, sine)
    grad_qvk, quarter_parts, sum_feed = both(grad_qvk, quarter_parts, sum_feed)
    ckv_share = summed([part[ROWS:] for part in quarter_parts]).astype(bf16)
    grad_attn, grad_qvk, ckv_share, sum_feed, sum_feed_far, feed_near = both(
        attn_products(
            full_one, grad_qvk, full_back, attended, own_context, ckv_share, full_two, grad_two_all, quarter_parts, att_quarter
        ),
        grad_qvk,
        ckv_share,
        sum_feed,
        to_far(sum_feed),
        gather_x(sum_feed),
    )
    parts_attn = plane_parts(grad_attn)
    half = 4 * ROWS
    blocks = halves_sum(dot_nt(grad_qvk[:half], w_qvk), dot_nt(grad_qvk[half:], w_qvk).astype(bf16))
    blocks, ckv_share, sum_feed_far, feed_near = both(blocks, ckv_share, sum_feed_far, feed_near)
    feed_all = [*feed_near, *gather_x(sum_feed_far)]
    cond_part = dot_nt(ckv_share, w_kv)[:cond_count]
    cond_part = (cond_part + to_partner(cond_part)).astype(bf16)
    grad_one, feed_parts = both(scatter_x(blocks), feed_parts)
    feed_branch = summed(feed_parts)
    output = resid_two + feed_branch
    sent_out = permuted(output.astype(bf16))
    in_grad = grad_resid_one + unit_norm_back(norm_one, scale_one, summed(grad_one))

    def columns_of(back):
        return lax.dynamic_slice_in_dim(cond_part, (x + 4 - back) % 4 * (D // 4), D // 4, 1)

    cond_parts = scatter_x([columns_of(back) for back in range(4)])
    cond_own = permuted(summed(cond_parts).astype(bf16))
    at = jnp.stack([x, yh]).astype(jnp.int32)

    def column(gain):
        return gain.astype(f32)[:, None]

    grad_feed_in, grad_feed_out = finish_feed(at, feed_all, column(gain_feed))

    def row_sums(w, grad):
        sums = jnp.sum(w.astype(f32) * grad.astype(f32), axis=1)
        return jnp.pad(sums, (0, 128 - half_rows))

    row = jnp.arange(own_rows, dtype=jnp.int32)
    valid = ((2 * x + tp) * own_rows + row < length)[:, None]
    squares = [jnp.sum(jnp.where(valid, v * v, 0.0)) for v in (tokens, attn_branch, cross_branch, feed_branch, output)]
    small = jnp.concatenate([row_sums(feed_cols, sum_feed[:, : 2 * hidden_quarter]), jnp.pad(jnp.stack(squares), (0, 123))])

    moved_in = lax.ppermute(permuted(in_grad.astype(bf16)), ("yh", "tp"), SWAP)
    moved_out = lax.ppermute(sent_out, ("yh", "tp"), SWAP)
    parts_attn, moved_in, moved_out, small, grad_feed_in, grad_feed_out = both(
        parts_attn, moved_in, moved_out, small, grad_feed_in, grad_feed_out
    )
    sum_attn = total(parts_attn)
    attn_own, cond_own = both(sum_attn.astype(bf16), cond_own)
    attn_near, attn_far, sum_attn, small, moved_in, moved_out, cond_own = both(
        gather_x(attn_own), to_far(attn_own), sum_attn, small, moved_in, moved_out, cond_own
    )
    attn_all = [*attn_near, *gather_x(attn_far)]
    cond_near = jnp.stack(gather_x(cond_own))
    more = [row_sums(qvk_cols, sum_attn[:, : 3 * quarter])]
    more += [row_sums(own_cols(cq_half, quarter), sum_attn[:, 6 * quarter : 7 * quarter])]
    small = sent_to_all(jnp.concatenate([*more, small])[None], ("x", "yh", "tp"), 16).reshape(4, 2, 2, 4, 128)
    in_grad = lax.all_gather(moved_in, "tp", axis=0, tiled=False).astype(f32)
    layer_out = lax.all_gather(moved_out, "tp", axis=0, tiled=False)
    cond_grad = finish_cond(at, cond_near, to_far(cond_near)).transpose(1, 0, 2)
    proj, out, keyval, query, cross = finish_columns(at, attn_all, column(gain_attn), column(gain_cross))
    small = jnp.sum(small, axis=(0, 2))
    layer_stats = jnp.sqrt(small[:, 3, :5] / (lengths.astype(f32)[:, None] * D))
    gains = [small[:, k, :half_rows].reshape(2 * half_rows) for k in range(3)]

    return (
        layer_out,
        in_grad,
        cond_grad,
        layer_stats,
        gains[0],
        proj.transpose(1, 0, 2),
        out,
        gains[1],
        query,
        keyval,
        cross,
        gains[2],
        grad_feed_in,
        grad_feed_out,
    )


def solution(mesh):
    fine = Mesh(mesh.devices.reshape(4, 2, 4, 2, 2), ("z", "yl", "x", "yh", "tp"))
    weights = (
        P(DP),
        P(DP, None, "tp"),
        P(DP, "tp"),
        P(DP),
        P(DP, "tp"),
        P(DP, None, "tp"),
        P(DP, "tp"),
        P(DP),
        P(DP, None, "tp"),
        P(DP, "tp"),
    )
    return jax.shard_map(
        per_device,
        mesh=fine,
        in_specs=(P(DP, CTX, None), P(DP, None, None), P(DP), P(DP, None), P(DP, CTX, None), *weights),
        out_specs=(P(DP, CTX, None), P(DP, CTX, None), P(DP, None, None), P(DP, None), *weights),
        check_vma=False,
    )
```
